512 devices in a mesh: sp: 64 (over z_hi, y, core), ch: 8 (over z_lo, x).
Axes of the slice: x: 4, y: 8, z: 8 (z_hi: 4, z_lo: 2; z = z_hi * 2 + z_lo), core: 2. Of those that a mesh axis runs over, the one named last changes fastest.
Arguments:
- image: bfloat16 [64, 4, 64, 768], P('sp', None, None, 'ch'), may hold values from -60 to 60
- cotangent: bfloat16 [64, 4, 64, 768], P('sp', None, None, 'ch'), may hold values from -6 to 6
- kernel: bfloat16 [7, 7, 768], P(None, None, 'ch'), may hold values from -0.875 to 0.875
- w_in: bfloat16 [768, 3072], P(None, 'ch'), may hold values from -0.21875 to 0.21875
- w_out: bfloat16 [3072, 768], P('ch'), may hold values from -0.109375 to 0.109375
Outputs:
- output: bfloat16 [64, 4, 64, 768], P('sp', None, None, 'ch')
- grad_image: bfloat16 [64, 4, 64, 768], P('sp', None, None, 'ch')
- grad_in: float32 [768, 3072], P(None, 'ch')
- grad_out: float32 [3072, 768], P('ch')
- grad_kernel: float32 [7, 7, 768], P(None, None, 'ch')
The draws below stay inside these ranges and needn't reach their ends.
All inputs are finite; a program needn't handle non-finite values.
Results may differ from the reference program's by a relative error of at most 0.015.
Values may be sent and summed in bfloat16 or wider, within the bound.
A program may use at most 64 MiB of HBM per device.

```python
import math
import jax
import jax.numpy as jnp
from jax import lax

C = 768
F = 3072
BLOCK_H = 4
BLOCK_W = 64
GRID_W = 8
BLOCKS = 64
N_CH = 8


def draw_image(key, part):
    base_key, chan_key, pixel_key = jax.random.split(jax.random.fold_in(key, 11), 3)
    shape = (BLOCKS, BLOCK_H, BLOCK_W, C)
    chan_scale = jnp.exp(jax.random.uniform(chan_key, (C,), jnp.float32, -0.5, 0.5) * math.log(10.0))
    pixel_scale = jnp.exp(jax.random.uniform(pixel_key, (BLOCKS, BLOCK_H, BLOCK_W, 1), jnp.float32, -0.5, 0.5) * math.log(10.0))
    base = jnp.clip(jax.random.normal(base_key, shape, jnp.float32), -6.0, 6.0)
    return (base * chan_scale * pixel_scale).astype(jnp.bfloat16)


def shard_levels(key, extent, cuts, low, largest):
    level = 1.0
    for axis_at, parts in cuts:
        heights = jax.random.uniform(jax.random.fold_in(jax.random.fold_in(key, 6), axis_at), (parts,), jnp.float32, low / len(cuts), largest / len(cuts))
        level = level * jnp.repeat(jnp.exp(heights), extent[axis_at] // parts).reshape((-1,) + (1,) * (len(extent) - 1 - axis_at))
    return level


def scatter_about(own_key, shape, deviation, reach, cuts=(), kind=jnp.bfloat16):
    array = deviation * jax.random.normal(own_key, shape, jnp.float32)
    if cuts:
        array = array * shard_levels(own_key, shape, cuts, -0.22, 0.18)
    return jnp.clip(array, -reach, reach).astype(kind)


def setup_inputs(seed: int = 0) -> dict:
    streams_of = jax.random.split(jax.random.key(seed), 6)
    return {
        "image": draw_image(jax.random.fold_in(streams_of[5], 71), 0),
        "cotangent": scatter_about(streams_of[1], (BLOCKS, BLOCK_H, BLOCK_W, C), 1.0, 6.0, ((0, 64), (3, 8))),
        "kernel": scatter_about(streams_of[2], (7, 7, C), 49 ** -0.5, 0.875, ((2, 8),)),
        "w_in": scatter_about(streams_of[3], (C, F), C ** -0.5, 0.21875, ((1, 8),)),
        "w_out": scatter_about(streams_of[4], (F, C), F ** -0.5, 0.109375, ((0, 8),)),
    }


def to_image(blocks):
    count, rows, cols, chans = blocks.shape
    grid = blocks.reshape(count // GRID_W, GRID_W, rows, cols, chans)
    return grid.transpose(0, 2, 1, 3, 4).reshape(count // GRID_W * rows, GRID_W * cols, chans)

def from_image(full):
    height, width, chans = full.shape
    rows = height // (BLOCKS // GRID_W)
    cols = width // GRID_W
    grid = full.reshape(BLOCKS // GRID_W, rows, GRID_W, cols, chans)
    return grid.transpose(0, 2, 1, 3, 4).reshape(BLOCKS, rows, cols, chans)

def reference(image, cotangent, kernel, w_in, w_out):
    pixels = to_image(image)
    grad_map = to_image(cotangent)
    height, width, chans = pixels.shape
    hidden = w_in.shape[1]
    panel_units = hidden // N_CH
    padded = jnp.pad(pixels, ((3, 3), (3, 3), (0, 0))).astype(jnp.float32)
    kernel_f = kernel.astype(jnp.float32)
    total = jnp.zeros((height, width, chans), jnp.float32)
    for row in range(7):
        for col in range(7):
            total = total + kernel_f[row, col] * padded[row:row + height, col:col + width]
    conv = total.astype(jnp.bfloat16)
    conv_f = conv.astype(jnp.float32)
    mean = lax.optimization_barrier(jnp.mean(conv_f, axis=-1, keepdims=True))
    var = lax.optimization_barrier(jnp.mean(conv_f * conv_f, axis=-1, keepdims=True)) - mean * mean
    rstd = lax.rsqrt(var + 1e-06)
    hat = (conv_f - mean) * rstd
    normed = hat.astype(jnp.bfloat16).reshape(-1, chans)
    pre = jnp.dot(normed, w_in, preferred_element_type=jnp.float32)
    act = (0.5 * pre * (1.0 + jax.scipy.special.erf(pre / jnp.sqrt(2.0)))).astype(jnp.bfloat16)
    branch = jnp.zeros((act.shape[0], chans), jnp.float32)
    for panel in range(N_CH):
        lo = panel * panel_units
        part_value = jnp.dot(act[:, lo:lo + panel_units], w_out[lo:lo + panel_units], preferred_element_type=jnp.float32)
        branch = branch + part_value.astype(jnp.bfloat16).astype(jnp.float32)
    branch = branch.reshape(height, width, chans)
    output = (pixels.astype(jnp.float32) + branch).astype(jnp.bfloat16)
    grad_flat = grad_map.reshape(-1, chans)
    d_act = jnp.dot(grad_flat, w_out.T, preferred_element_type=jnp.float32)
    grad_out = jnp.dot(act.T, grad_flat, preferred_element_type=jnp.float32)
    slope = 0.5 * (1.0 + jax.scipy.special.erf(pre / jnp.sqrt(2.0))) + pre * jnp.exp(-0.5 * pre * pre) / jnp.sqrt(2.0 * jnp.pi)
    d_pre = (d_act * slope).astype(jnp.bfloat16)
    grad_in = jnp.dot(normed.T, d_pre, preferred_element_type=jnp.float32)
    d_norm = jnp.zeros((d_pre.shape[0], chans), jnp.float32)
    for panel in range(N_CH):
        lo = panel * panel_units
        part_value = jnp.dot(d_pre[:, lo:lo + panel_units], w_in[:, lo:lo + panel_units].T, preferred_element_type=jnp.float32)
        d_norm = d_norm + part_value.astype(jnp.bfloat16).astype(jnp.float32)
    d_norm = d_norm.reshape(height, width, chans)
    first = lax.optimization_barrier(jnp.sum(d_norm, axis=-1, keepdims=True))
    second = lax.optimization_barrier(jnp.sum(d_norm * hat, axis=-1, keepdims=True))
    d_conv = (rstd * (d_norm - first / chans - hat * second / chans)).astype(jnp.bfloat16)
    d_conv_f = d_conv.astype(jnp.float32)
    taps = []
    for row in range(7):
        for col in range(7):
            taps.append(lax.optimization_barrier(jnp.sum(d_conv_f * padded[row:row + height, col:col + width], axis=(0, 1))))
    grad_kernel = jnp.stack(taps).reshape(7, 7, chans)
    d_padded = jnp.pad(d_conv_f, ((3, 3), (3, 3), (0, 0)))
    back = grad_map.astype(jnp.float32)
    for row in range(7):
        for col in range(7):
            back = back + kernel_f[row, col] * d_padded[6 - row:6 - row + height, 6 - col:6 - col + width]
    grad_image = back.astype(jnp.bfloat16)
    return (from_image(output), from_image(grad_image), grad_in, grad_out, grad_kernel)
```

```python
import jax
import jax.numpy as jnp
from jax import lax
from jax.experimental import pallas as pl
from jax.experimental.pallas import tpu as pltpu
from jax.sharding import PartitionSpec as P

GRID_W = 8
MESH = pl.DeviceIdType.MESH
DIRS = ((-1, 0), (1, 0), (0, -1), (0, 1), (-1, -1), (-1, 1), (1, -1), (1, 1))
LEFT = 8
F32 = jnp.float32
BF16 = jnp.bfloat16


def greet(peers):
    barrier = pltpu.get_barrier_semaphore()
    for peer in peers:
        pl.semaphore_signal(barrier, inc=1, device_id=peer, device_id_type=MESH)
    pl.semaphore_wait(barrier, len(peers))


def send(src, dst, send_sem, recv_sem, peer):
    copy = pltpu.make_async_remote_copy(
        src_ref=src,
        dst_ref=dst,
        send_sem=send_sem,
        recv_sem=recv_sem,
        device_id=peer,
        device_id_type=MESH,
    )
    copy.start()
    return copy


def call(body, name, cid, out_shape, scratch):
    def run(*args):
        return pl.pallas_call(
            body,
            out_shape=out_shape,
            in_specs=[pl.BlockSpec(memory_space=pltpu.VMEM)] * len(args),
            out_specs=tuple([pl.BlockSpec(memory_space=pltpu.VMEM)] * len(out_shape)),
            scratch_shapes=scratch,
            compiler_params=pltpu.CompilerParams(
                collective_id=cid, has_side_effects=True, vmem_limit_bytes=48 * 2**20
            ),
            name=name,
        )(*args)

    return run


def shape(dims, dtype):
    return jax.ShapeDtypeStruct(dims, dtype)


def cut(block, dr, dc):
    if dr:
        block = block[:3] if dr < 0 else block[-3:]
    if dc:
        block = block[:, :3] if dc < 0 else block[:, -3:]
    return block


def strips(block):
    return [cut(block, dr, dc) for dr, dc in DIRS]


def start_margins(srcs, lands, send_sem, recv_sem):
    b, ch = lax.axis_index("sp"), lax.axis_index("ch")
    row, col = b // GRID_W, b % GRID_W
    peers = []
    for dr, dc in DIRS:
        r = lax.rem(row + dr + GRID_W, GRID_W)
        c = lax.rem(col + dc + GRID_W, GRID_W)
        peers.append((r * GRID_W + c, ch))
    greet(peers)
    return [
        send(srcs[k], lands[k], send_sem.at[k], recv_sem.at[k], peers[k]) for k in range(8)
    ]


def fill_margins(pad, block, lands):
    b = lax.axis_index("sp")
    row, col = b // GRID_W, b % GRID_W
    rows, cols = block.shape[0], block.shape[1]
    pad[3 : 3 + rows, LEFT : LEFT + cols] = block[...].astype(F32)
    for k, (dr, dc) in enumerate(DIRS):
        keep = jnp.logical_and(
            jnp.logical_and(row - dr >= 0, row - dr < GRID_W),
            jnp.logical_and(col - dc >= 0, col - dc < GRID_W),
        )
        value = lands[k][...].astype(F32)
        value = value * jnp.where(keep, 1.0, 0.0).astype(F32)
        top = 3 if dr == 0 else (0 if dr > 0 else 3 + rows)
        left = LEFT if dc == 0 else (LEFT - 3 if dc > 0 else LEFT + cols)
        pad[top : top + value.shape[0], left : left + value.shape[1]] = value


def front_kernel(*refs):
    block, taps = refs[0], refs[1]
    srcs = refs[2:10]
    conv, pad = refs[10], refs[11]
    lands, send_sem, recv_sem = refs[12:20], refs[20], refs[21]
    rows, cols = block.shape[0], block.shape[1]
    copies = start_margins(srcs, lands, send_sem, recv_sem)
    pad[...] = jnp.zeros_like(pad)
    for copy in copies:
        copy.wait()
    fill_margins(pad, block, lands)
    for p in range(rows):
        total = jnp.zeros(block.shape[1:], F32)
        for i in range(7):
            for j in range(7):
                t = i * 7 + j
                start = LEFT - 3 + j
                total = total + taps[t : t + 1, :] * pad[p + i, start : start + cols, :]
        conv[p] = total.astype(BF16)


def back_kernel(*refs):
    block, taps, grad_map, pad_x = refs[0:4]
    srcs = refs[4:12]
    grad_image, grad_taps = refs[12], refs[13]
    lands, pad, send_sem, recv_sem = refs[14:22], refs[22], refs[23], refs[24]
    rows, cols = block.shape[0], block.shape[1]
    copies = start_margins(srcs, lands, send_sem, recv_sem)
    pad[...] = jnp.zeros_like(pad)
    grad_taps[...] = jnp.zeros_like(grad_taps)
    for i in range(7):
        for j in range(7):
            t = i * 7 + j
            start = LEFT - 3 + j
            total = jnp.zeros(block.shape[1:], F32)
            for p in range(rows):
                total = total + block[p].astype(F32) * pad_x[p + i, start : start + cols, :]
            grad_taps[t : t + 1, :] = jnp.sum(total, axis=0, keepdims=True)
    for copy in copies:
        copy.wait()
    fill_margins(pad, block, lands)
    for p in range(rows):
        total = grad_map[p].astype(F32)
        for i in range(7):
            for j in range(7):
                t = i * 7 + j
                start = LEFT + 3 - j
                total = total + taps[t : t + 1, :] * pad[p + 6 - i, start : start + cols, :]
        grad_image[p] = total.astype(BF16)


def ch_peers(n):
    b, me = lax.axis_index("sp"), lax.axis_index("ch")
    return me, [(b, lax.rem(me + d, n)) for d in range(1, n)]


def send_stats(stat, me, peers, first, second, send_sem, recv_sem):
    stat[me, 0:1, :] = first
    stat[me, 1:2, :] = second
    return [
        send(stat.at[me], stat.at[me], send_sem.at[d], recv_sem.at[d], peer)
        for d, peer in enumerate(peers)
    ]


def sum_stats(stat, copies):
    for copy in copies:
        copy.wait()
    total = stat[0]
    for k in range(1, stat.shape[0]):
        total = total + stat[k]
    return total[0:1], total[1:2]


def gather_kernel(
    conv, grad_map, normed_all, grad_all, hat, rstd, stat, ssem, rsem
):
    n, panel, _ = normed_all.shape
    me, peers = ch_peers(n)
    chans = n * panel
    stat[me] = jnp.zeros(stat.shape[1:], F32)
    greet(peers)
    value = conv[...].astype(F32)
    stats = send_stats(
        stat,
        me,
        peers,
        jnp.sum(value, axis=0, keepdims=True),
        jnp.sum(value * value, axis=0, keepdims=True),
        ssem.at[0],
        rsem.at[0],
    )
    grads = [
        send(grad_map, grad_all.at[me], ssem.at[1, d], rsem.at[1, d], peer)
        for d, peer in enumerate(peers)
    ]
    grad_all[me] = grad_map[...]
    first, second = sum_stats(stat, stats)
    mean = first / chans
    var = second / chans - mean * mean
    scale = lax.rsqrt(var + 1e-06)
    rstd[...] = scale
    local = (value - mean) * scale
    hat[...] = local
    normed_all[me] = local.astype(BF16)
    outs = [
        send(normed_all.at[me], normed_all.at[me], ssem.at[2, d], rsem.at[2, d], peer)
        for d, peer in enumerate(peers)
    ]
    for copy in grads + outs:
        copy.wait()


def scatter_kernel(
    part_out, part_norm, hat, rstd, image, output, d_conv, land, stat, ssem, rsem
):
    n, panel, _ = part_out.shape
    me, peers = ch_peers(n)
    chans = n * panel
    stat[me] = jnp.zeros(stat.shape[1:], F32)
    greet(peers)
    norms = [
        send(part_norm.at[peer[1]], land.at[0, d], ssem.at[0, d], rsem.at[0, d], peer)
        for d, peer in enumerate(peers)
    ]
    outs = [
        send(part_out.at[peer[1]], land.at[1, d], ssem.at[1, d], rsem.at[1, d], peer)
        for d, peer in enumerate(peers)
    ]
    d_norm = part_norm[me].astype(F32)
    for d, copy in enumerate(norms):
        copy.wait()
        d_norm = d_norm + land[0, d].astype(F32)
    local = hat[...]
    stats = send_stats(
        stat,
        me,
        peers,
        jnp.sum(d_norm, axis=0, keepdims=True),
        jnp.sum(d_norm * local, axis=0, keepdims=True),
        ssem.at[2],
        rsem.at[2],
    )
    branch = part_out[me].astype(F32)
    for d, copy in enumerate(outs):
        copy.wait()
        branch = branch + land[1, d].astype(F32)
    output[...] = (image[...].astype(F32) + branch).astype(BF16)
    first, second = sum_stats(stat, stats)
    d_conv[...] = (
        rstd[...] * (d_norm - first / chans - local * second / chans)
    ).astype(BF16)


def reduce_kernel(
    grads, taps, out, taps_out, land0, tland0, mine, tmine, land1, tland1, land2, tland2, ssem, rsem
):
    b, ch = lax.axis_index("sp"), lax.axis_index("ch")
    ny, nz = grads.shape[1], land2.shape[0]
    core, y, z = b % 2, (b // 2) % ny, b // (2 * ny)
    other = (b + 1 - 2 * core, ch)
    ys = [lax.rem(y + d, ny) for d in range(1, ny)]
    zs = [lax.rem(z + d, nz) for d in range(1, nz)]
    y_peers = [((z * ny + k) * 2 + core, ch) for k in ys]
    z_peers = [((k * ny + y) * 2 + core, ch) for k in zs]
    greet([other] + y_peers + z_peers)

    firsts = [
        send(grads.at[1 - core, k], land0.at[k], ssem.at[0, k], rsem.at[0, k], other)
        for k in range(ny)
    ]
    tfirst = send(taps, tland0, ssem.at[1, 0], rsem.at[1, 0], other)
    tfirst.wait()
    tmine[...] = taps[...] + tland0[...]
    for k in range(ny):
        firsts[k].wait()
        mine[k] = (grads[core, k].astype(F32) + land0[k].astype(F32)).astype(BF16)

    moves, tmoves = [], []
    for d in range(ny - 1):
        moves.append(
            send(mine.at[ys[d]], land1.at[d], ssem.at[2, d], rsem.at[2, d], y_peers[d])
        )
        tmoves.append(
            send(tmine.at[ys[d]], tland1.at[d], ssem.at[3, d], rsem.at[3, d], y_peers[d])
        )
    total, ttotal = mine[y].astype(F32), tmine[y]
    for d in range(ny - 1):
        moves[d].wait()
        tmoves[d].wait()
        total = total + land1[d].astype(F32)
        ttotal = ttotal + tland1[d]
    land2[z] = total.astype(BF16)
    tland2[z] = ttotal

    moves, tmoves = [], []
    for d in range(nz - 1):
        moves.append(send(land2.at[z], land2.at[z], ssem.at[4, d], rsem.at[4, d], z_peers[d]))
        tmoves.append(send(tland2.at[z], tland2.at[z], ssem.at[5, d], rsem.at[5, d], z_peers[d]))
    for copy in moves + tmoves:
        copy.wait()
    total, ttotal = land2[0].astype(F32), tland2[0]
    for k in range(1, nz):
        total = total + land2[k].astype(F32)
        ttotal = ttotal + tland2[k]
    out[core, y] = total.astype(BF16)
    taps_out[y] = ttotal

    moves, tmoves, pairs = [], [], []
    for d in range(ny - 1):
        moves.append(
            send(out.at[core, y], out.at[core, y], ssem.at[6, d], rsem.at[6, d], y_peers[d])
        )
        tmoves.append(
            send(taps_out.at[y], taps_out.at[y], ssem.at[7, d], rsem.at[7, d], y_peers[d])
        )
    pairs.append(send(out.at[core, y], out.at[core, y], ssem.at[8, 0], rsem.at[8, 0], other))
    for d in range(ny - 1):
        moves[d].wait()
        k = lax.rem(y - d - 1 + ny, ny)
        pairs.append(
            send(out.at[core, k], out.at[core, k], ssem.at[8, d + 1], rsem.at[8, d + 1], other)
        )
    for copy in tmoves + pairs:
        copy.wait()


def make_shards(ny, nz):
    def shards(image, cotangent, kernel, w_in, w_out):
        block, grad_map = image[0], cotangent[0]
        rows, cols, panel = block.shape
        pixels = rows * cols
        n = w_in.shape[0] // panel
        hidden = w_in.shape[1]
        chans = w_in.shape[0]
        taps = kernel.astype(F32).reshape(49, panel)
        lands = [pltpu.VMEM(s.shape, BF16) for s in strips(block)]
        sems = [pltpu.SemaphoreType.DMA((8,)), pltpu.SemaphoreType.DMA((8,))]
        padded = (rows + 6, cols + 2 * LEFT, panel)

        conv, pad_x = call(
            front_kernel,
            "front",
            1,
            (shape(block.shape, BF16), shape(padded, F32)),
            lands + sems,
        )(block, taps, *strips(block))

        conv_t = conv.reshape(pixels, panel).T
        grad_t = grad_map.reshape(pixels, panel).T
        image_t = block.reshape(pixels, panel).T
        all_dims = (n, panel, pixels)
        normed_t, gall_t, hat, rstd = call(
            gather_kernel,
            "gather",
            2,
            (
                shape(all_dims, BF16),
                shape(all_dims, BF16),
                shape((panel, pixels), F32),
                shape((1, pixels), F32),
            ),
            [
                pltpu.VMEM((n, 8, pixels), F32),
                pltpu.SemaphoreType.DMA((3, n - 1)),
                pltpu.SemaphoreType.DMA((3, n - 1)),
            ],
        )(conv_t, grad_t)
        normed_t = normed_t.reshape(chans, pixels)
        gall_t = gall_t.reshape(chans, pixels)

        def mm(a, b, dims):
            return lax.dot_general(a, b, (dims, ((), ())), preferred_element_type=F32)

        pre = mm(w_in, normed_t, ((0,), (0,)))
        half = 0.5 * (1.0 + jax.scipy.special.erf(pre / jnp.sqrt(2.0)))
        act = (pre * half).astype(BF16)
        slope = half + pre * jnp.exp(-0.5 * pre * pre) / jnp.sqrt(2.0 * jnp.pi)
        d_act = mm(w_out, gall_t, ((1,), (0,)))
        d_pre = (d_act * slope).astype(BF16)
        part_out = mm(w_out, act, ((0,), (0,))).astype(BF16)
        part_norm = mm(w_in, d_pre, ((1,), (0,))).astype(BF16)
        grad_in = mm(normed_t, d_pre, ((1,), (1,))).astype(BF16)
        grad_out_t = mm(gall_t, act, ((1,), (1,))).astype(BF16)

        out_t, d_conv_t = call(
            scatter_kernel,
            "scatter",
            3,
            (shape((panel, pixels), BF16), shape((panel, pixels), BF16)),
            [
                pltpu.VMEM((2, n - 1, panel, pixels), BF16),
                pltpu.VMEM((n, 8, pixels), F32),
                pltpu.SemaphoreType.DMA((3, n - 1)),
                pltpu.SemaphoreType.DMA((3, n - 1)),
            ],
        )(part_out.reshape(all_dims), part_norm.reshape(all_dims), hat, rstd, image_t)
        output = out_t.T.reshape(block.shape)
        d_conv = d_conv_t.T.reshape(block.shape)

        grad_image, grad_taps = call(
            back_kernel,
            "back",
            4,
            (shape(block.shape, BF16), shape((56, panel), F32)),
            lands + [pltpu.VMEM(padded, F32)] + sems,
        )(d_conv, taps, grad_map, pad_x, *strips(d_conv))

        flat = grad_taps[:49].reshape(-1)
        flat = jnp.pad(flat, (0, ny * 8 * 128 - flat.shape[0])).reshape(ny, 8, 128)
        piece = chans // ny
        grads = jnp.stack([grad_in, grad_out_t]).reshape(2, ny, piece, hidden)
        total, taps_total = call(
            reduce_kernel,
            "reduce",
            5,
            (shape(grads.shape, BF16), shape(flat.shape, F32)),
            [
                pltpu.VMEM((ny, piece, hidden), BF16),
                pltpu.VMEM(flat.shape, F32),
                pltpu.VMEM((ny, piece, hidden), BF16),
                pltpu.VMEM(flat.shape, F32),
                pltpu.VMEM((ny - 1, piece, hidden), BF16),
                pltpu.VMEM((ny - 1, 8, 128), F32),
                pltpu.VMEM((nz, piece, hidden), BF16),
                pltpu.VMEM((nz, 8, 128), F32),
                pltpu.SemaphoreType.DMA((9, ny)),
                pltpu.SemaphoreType.DMA((9, ny)),
            ],
        )(grads, flat)
        total = total.astype(F32).reshape(2, chans, hidden)
        grad_kernel = taps_total.reshape(-1)[: 49 * panel].reshape(7, 7, panel)
        return output[None], grad_image[None], total[0], total[1].T, grad_kernel

    return shards


def solution(mesh):
    ny = 8
    nz = mesh.shape["sp"] // (2 * ny)
    return jax.shard_map(
        make_shards(ny, nz),
        mesh=mesh,
        in_specs=(
            P("sp", None, None, "ch"),
            P("sp", None, None, "ch"),
            P(None, None, "ch"),
            P(None, "ch"),
            P("ch", None),
        ),
        out_specs=(
            P("sp", None, None, "ch"),
            P("sp", None, None, "ch"),
            P(None, "ch"),
            P("ch", None),
            P(None, None, "ch"),
        ),
        check_vma=False,
    )
```

```python
import jax
import jax.numpy as jnp
from jax import lax
from jax.experimental import pallas as pl
from jax.experimental.pallas import tpu as pltpu
from jax.sharding import PartitionSpec as P

GRID_W = 8
MESH = pl.DeviceIdType.MESH
DIRS = ((-1, 0), (1, 0), (0, -1), (0, 1), (-1, -1), (-1, 1), (1, -1), (1, 1))
EDGE = 16
LEFT = 8
F32 = jnp.float32
BF16 = jnp.bfloat16


def greet(peers):
    barrier = pltpu.get_barrier_semaphore()
    for peer in peers:
        pl.semaphore_signal(barrier, inc=1, device_id=peer, device_id_type=MESH)
    pl.semaphore_wait(barrier, len(peers))


def send(src, dst, send_sem, recv_sem, peer):
    copy = pltpu.make_async_remote_copy(
        src_ref=src,
        dst_ref=dst,
        send_sem=send_sem,
        recv_sem=recv_sem,
        device_id=peer,
        device_id_type=MESH,
    )
    copy.start()
    return copy


def call(body, name, cid, out_shape, scratch):
    def run(*args):
        return pl.pallas_call(
            body,
            out_shape=out_shape,
            in_specs=[pl.BlockSpec(memory_space=pltpu.VMEM)] * len(args),
            out_specs=tuple([pl.BlockSpec(memory_space=pltpu.VMEM)] * len(out_shape)),
            scratch_shapes=scratch,
            compiler_params=pltpu.CompilerParams(
                collective_id=cid, has_side_effects=True, vmem_limit_bytes=48 * 2**20
            ),
            name=name,
        )(*args)

    return run


def shape(dims, dtype):
    return jax.ShapeDtypeStruct(dims, dtype)


def window(dr, dc, rows, cols):
    r = slice(0, rows) if dr == 0 else (slice(0, 3) if dr < 0 else slice(rows - 3, rows))
    c = slice(0, cols) if dc == 0 else (slice(0, EDGE) if dc < 0 else slice(cols - EDGE, cols))
    return r, c


def margin_peers():
    b, ch = lax.axis_index("sp"), lax.axis_index("ch")
    row, col = b // GRID_W, b % GRID_W
    peers = []
    for dr, dc in DIRS:
        r = lax.rem(row + dr + GRID_W, GRID_W)
        c = lax.rem(col + dc + GRID_W, GRID_W)
        peers.append((r * GRID_W + c, ch))
    return peers


def start_margins(block, lands, send_sem, recv_sem, peers):
    rows, cols = block.shape[0], block.shape[1]
    copies = []
    for k, (dr, dc) in enumerate(DIRS):
        r, c = window(dr, dc, rows, cols)
        copies.append(
            send(block.at[r, c], lands[k], send_sem.at[k], recv_sem.at[k], peers[k])
        )
    return copies


def fill_margins(pad, block, lands):
    b = lax.axis_index("sp")
    row, col = b // GRID_W, b % GRID_W
    rows, cols = block.shape[0], block.shape[1]
    pad[3 : 3 + rows, LEFT : LEFT + cols] = block[...].astype(F32)
    for k, (dr, dc) in enumerate(DIRS):
        keep = jnp.logical_and(
            jnp.logical_and(row - dr >= 0, row - dr < GRID_W),
            jnp.logical_and(col - dc >= 0, col - dc < GRID_W),
        )
        value = lands[k][...].astype(F32)
        value = value * jnp.where(keep, 1.0, 0.0).astype(F32)
        if dc:
            value = value[:, :3] if dc < 0 else value[:, EDGE - 3 :]
        top = 3 if dr == 0 else (0 if dr > 0 else 3 + rows)
        left = LEFT if dc == 0 else (LEFT - 3 if dc > 0 else LEFT + cols)
        pad[top : top + value.shape[0], left : left + value.shape[1]] = value


def ch_peers(n):
    b, me = lax.axis_index("sp"), lax.axis_index("ch")
    return me, [(b, lax.rem(me + d, n)) for d in range(1, n)]


def send_stats(stat, me, peers, first, second, send_sem, recv_sem):
    stat[me, 0:1, :] = first
    stat[me, 1:2, :] = second
    return [
        send(stat.at[me], stat.at[me], send_sem.at[d], recv_sem.at[d], peer)
        for d, peer in enumerate(peers)
    ]


def sum_stats(stat, copies):
    for copy in copies:
        copy.wait()
    total = stat[0]
    for k in range(1, stat.shape[0]):
        total = total + stat[k]
    return total[0:1], total[1:2]


def to_channels(wide, panel):
    return wide[...].T[0:panel]


def to_pixels(tall, value, dims):
    rows, cols, panel = dims
    tall[0:panel, :] = value
    turned = tall[...].T
    return [turned[p * cols : (p + 1) * cols, 0:panel] for p in range(rows)]


def front_kernel(*refs):
    block, taps, grad_map = refs[0:3]
    normed_all, grad_all, hat, rstd, pad = refs[3:8]
    lands, msem, mrsem = refs[8:16], refs[16], refs[17]
    wide, stat, ssem, rsem = refs[18:22]
    rows, cols, panel = block.shape
    n = normed_all.shape[0]
    chans = n * panel
    me, peers = ch_peers(n)
    near = margin_peers()
    stat[me] = jnp.zeros(stat.shape[1:], F32)
    wide[...] = jnp.zeros_like(wide)
    for p in range(rows):
        wide[p * cols : (p + 1) * cols, 0:panel] = grad_map[p].astype(F32)
    grad_all[me] = to_channels(wide, panel).astype(BF16)
    greet(near + peers)
    copies = start_margins(block, lands, msem, mrsem, near)
    grads = [
        send(grad_all.at[me], grad_all.at[me], ssem.at[1, d], rsem.at[1, d], peer)
        for d, peer in enumerate(peers)
    ]
    pad[...] = jnp.zeros_like(pad)
    for copy in copies:
        copy.wait()
    fill_margins(pad, block, lands)
    for p in range(rows):
        total = jnp.zeros(block.shape[1:], F32)
        for i in range(7):
            for j in range(7):
                t = i * 7 + j
                start = LEFT - 3 + j
                total = total + taps[t : t + 1, :] * pad[p + i, start : start + cols, :]
        wide[p * cols : (p + 1) * cols, 0:panel] = total.astype(BF16).astype(F32)
    value = to_channels(wide, panel)
    stats = send_stats(
        stat,
        me,
        peers,
        jnp.sum(value, axis=0, keepdims=True),
        jnp.sum(value * value, axis=0, keepdims=True),
        ssem.at[0],
        rsem.at[0],
    )
    first, second = sum_stats(stat, stats)
    mean = first / chans
    var = second / chans - mean * mean
    scale = lax.rsqrt(var + 1e-06)
    rstd[...] = scale
    local = (value - mean) * scale
    hat[...] = local
    normed_all[me] = local.astype(BF16)
    outs = [
        send(normed_all.at[me], normed_all.at[me], ssem.at[2, d], rsem.at[2, d], peer)
        for d, peer in enumerate(peers)
    ]
    for copy in grads + outs:
        copy.wait()


def back_kernel(*refs):
    part_out, part_norm, hat, rstd, image, grad_map, taps, pad_x, grads = refs[0:9]
    output, grad_image, out, taps_out = refs[9:13]
    lands, msem, mrsem = refs[13:21], refs[21], refs[22]
    land, stat, csem, crsem, tall, d_conv, pad, mytaps = refs[23:31]
    land0, mine, land1, land2, tland0, tmine, tland1, tland2, ssem, rsem = refs[31:41]

    n, panel, pixels = part_out.shape
    rows, cols, _ = image.shape
    chans = n * panel
    b, ch = lax.axis_index("sp"), lax.axis_index("ch")
    me, peers = ch_peers(n)
    near = margin_peers()
    ny, nz = grads.shape[1], land2.shape[0]
    core, y, z = b % 2, (b // 2) % ny, b // (2 * ny)
    other = (b + 1 - 2 * core, ch)
    ys = [lax.rem(y + d, ny) for d in range(1, ny)]
    zs = [lax.rem(z + d, nz) for d in range(1, nz)]
    y_peers = [((z * ny + k) * 2 + core, ch) for k in ys]
    z_peers = [((k * ny + y) * 2 + core, ch) for k in zs]
    stat[me] = jnp.zeros(stat.shape[1:], F32)
    greet(peers + near + [other] + y_peers + z_peers)

    norms = [
        send(part_norm.at[peer[1]], land.at[0, d], csem.at[0, d], crsem.at[0, d], peer)
        for d, peer in enumerate(peers)
    ]
    outs = [
        send(part_out.at[peer[1]], land.at[1, d], csem.at[1, d], crsem.at[1, d], peer)
        for d, peer in enumerate(peers)
    ]
    order = ys + [y]
    firsts = [
        send(grads.at[1 - core, k], land0.at[k], ssem.at[0, d], rsem.at[0, d], other)
        for d, k in enumerate(order)
    ]
    tall[...] = jnp.zeros_like(tall)
    mytaps[...] = jnp.zeros_like(mytaps)
    pad[...] = jnp.zeros_like(pad)

    moves = []
    for d, k in enumerate(order):
        firsts[d].wait()
        mine[k] = (grads[core, k].astype(F32) + land0[k].astype(F32)).astype(BF16)
        if d < ny - 1:
            moves.append(
                send(mine.at[k], land1.at[d], ssem.at[2, d], rsem.at[2, d], y_peers[d])
            )

    d_norm = part_norm[me].astype(F32)
    for d, copy in enumerate(norms):
        copy.wait()
        d_norm = d_norm + land[0, d].astype(F32)
    local = hat[...]
    stats = send_stats(
        stat,
        me,
        peers,
        jnp.sum(d_norm, axis=0, keepdims=True),
        jnp.sum(d_norm * local, axis=0, keepdims=True),
        csem.at[2],
        crsem.at[2],
    )
    branch = part_out[me].astype(F32)
    for d, copy in enumerate(outs):
        copy.wait()
        branch = branch + land[1, d].astype(F32)
    for p, value in enumerate(to_pixels(tall, branch, image.shape)):
        output[p] = (image[p].astype(F32) + value).astype(BF16)
    first, second = sum_stats(stat, stats)
    back = rstd[...] * (d_norm - first / chans - local * second / chans)
    for p, value in enumerate(to_pixels(tall, back, image.shape)):
        d_conv[p] = value.astype(BF16)
    margins = start_margins(d_conv, lands, msem, mrsem, near)

    for i in range(7):
        for j in range(7):
            t = i * 7 + j
            start = LEFT - 3 + j
            total = jnp.zeros(image.shape[1:], F32)
            for p in range(rows):
                total = total + d_conv[p].astype(F32) * pad_x[p + i, start : start + cols, :]
            mytaps[t // 8, t % 8 : t % 8 + 1, 0:panel] = jnp.sum(total, axis=0, keepdims=True)
    tfirst = send(mytaps, tland0, ssem.at[1, 0], rsem.at[1, 0], other)

    total = mine[y].astype(F32)
    for d in range(ny - 1):
        moves[d].wait()
        total = total + land1[d].astype(F32)
    land2[z] = total.astype(BF16)
    moves = [
        send(land2.at[z], land2.at[z], ssem.at[4, d], rsem.at[4, d], z_peers[d])
        for d in range(nz - 1)
    ]

    tfirst.wait()
    tmine[...] = mytaps[...] + tland0[...]
    tmoves = [
        send(tmine.at[ys[d]], tland1.at[d], ssem.at[3, d], rsem.at[3, d], y_peers[d])
        for d in range(ny - 1)
    ]

    for copy in margins:
        copy.wait()
    fill_margins(pad, d_conv, lands)
    for p in range(rows):
        total = grad_map[p].astype(F32)
        for i in range(7):
            for j in range(7):
                t = i * 7 + j
                start = LEFT + 3 - j
                total = total + taps[t : t + 1, :] * pad[p + 6 - i, start : start + cols, :]
        grad_image[p] = total.astype(BF16)

    for copy in moves:
        copy.wait()
    total = land2[0].astype(F32)
    for k in range(1, nz):
        total = total + land2[k].astype(F32)
    out[core, y] = total.astype(BF16)
    moves = [
        send(out.at[core, y], out.at[core, y], ssem.at[6, d], rsem.at[6, d], y_peers[d])
        for d in range(ny - 1)
    ]
    pairs = [send(out.at[core, y], out.at[core, y], ssem.at[8, 0], rsem.at[8, 0], other)]

    ttotal = tmine[y]
    for d in range(ny - 1):
        tmoves[d].wait()
        ttotal = ttotal + tland1[d]
    tland2[z] = ttotal
    tmoves = [
        send(tland2.at[z], tland2.at[z], ssem.at[5, d], rsem.at[5, d], z_peers[d])
        for d in range(nz - 1)
    ]
    for copy in tmoves:
        copy.wait()
    ttotal = tland2[0]
    for k in range(1, nz):
        ttotal = ttotal + tland2[k]
    taps_out[y] = ttotal
    tmoves = [
        send(taps_out.at[y], taps_out.at[y], ssem.at[7, d], rsem.at[7, d], y_peers[d])
        for d in range(ny - 1)
    ]

    for d in range(ny - 1):
        moves[d].wait()
        k = lax.rem(y - d - 1 + ny, ny)
        pairs.append(
            send(out.at[core, k], out.at[core, k], ssem.at[8, d + 1], rsem.at[8, d + 1], other)
        )
    for copy in tmoves + pairs:
        copy.wait()


def make_shards(ny, nz):
    def shards(image, cotangent, kernel, w_in, w_out):
        block, grad_map = image[0], cotangent[0]
        rows, cols, panel = block.shape
        pixels = rows * cols
        n = w_in.shape[0] // panel
        hidden = w_in.shape[1]
        chans = w_in.shape[0]
        taps = kernel.astype(F32).reshape(49, panel)
        lands = []
        for dr, dc in DIRS:
            lands.append(
                pltpu.VMEM((3 if dr else rows, EDGE if dc else cols, panel), BF16)
            )

        def sems(*dims):
            return [pltpu.SemaphoreType.DMA(dims), pltpu.SemaphoreType.DMA(dims)]

        padded = (rows + 6, cols + 2 * LEFT, panel)
        all_dims = (n, panel, pixels)
        normed_t, gall_t, hat, rstd, pad_x = call(
            front_kernel,
            "front",
            1,
            (
                shape(all_dims, BF16),
                shape(all_dims, BF16),
                shape((panel, pixels), F32),
                shape((1, pixels), F32),
                shape(padded, F32),
            ),
            lands
            + sems(8)
            + [pltpu.VMEM((pixels, 128), F32), pltpu.VMEM((n, 8, pixels), F32)]
            + sems(3, n - 1),
        )(block, taps, grad_map)
        normed_t = normed_t.reshape(chans, pixels)
        gall_t = gall_t.reshape(chans, pixels)

        def mm(a, b, dims):
            return lax.dot_general(a, b, (dims, ((), ())), preferred_element_type=F32)

        pre = mm(w_in, normed_t, ((0,), (0,)))
        half = 0.5 * (1.0 + jax.scipy.special.erf(pre / jnp.sqrt(2.0)))
        act = (pre * half).astype(BF16)
        slope = half + pre * jnp.exp(-0.5 * pre * pre) / jnp.sqrt(2.0 * jnp.pi)
        d_act = mm(w_out, gall_t, ((1,), (0,)))
        d_pre = (d_act * slope).astype(BF16)
        part_out = mm(w_out, act, ((0,), (0,))).astype(BF16)
        part_norm = mm(w_in, d_pre, ((1,), (0,))).astype(BF16)
        grad_in = mm(normed_t, d_pre, ((1,), (1,))).astype(BF16)
        grad_out_t = mm(gall_t, act, ((1,), (1,))).astype(BF16)

        piece = chans // ny
        grads = jnp.stack([grad_in, grad_out_t]).reshape(2, ny, piece, hidden)
        tdims = (ny, 8, 128)
        output, grad_image, total, taps_total = call(
            back_kernel,
            "back",
            2,
            (
                shape(block.shape, BF16),
                shape(block.shape, BF16),
                shape(grads.shape, BF16),
                shape(tdims, F32),
            ),
            lands
            + sems(8)
            + [pltpu.VMEM((2, n - 1, panel, pixels), BF16), pltpu.VMEM((n, 8, pixels), F32)]
            + sems(3, n - 1)
            + [
                pltpu.VMEM((128, pixels), F32),
                pltpu.VMEM(block.shape, BF16),
                pltpu.VMEM(padded, F32),
                pltpu.VMEM(tdims, F32),
                pltpu.VMEM((ny, piece, hidden), BF16),
                pltpu.VMEM((ny, piece, hidden), BF16),
                pltpu.VMEM((ny - 1, piece, hidden), BF16),
                pltpu.VMEM((nz, piece, hidden), BF16),
                pltpu.VMEM(tdims, F32),
                pltpu.VMEM(tdims, F32),
                pltpu.VMEM((ny - 1, 8, 128), F32),
                pltpu.VMEM((nz, 8, 128), F32),
            ]
            + sems(9, ny),
        )(
            part_out.reshape(all_dims),
            part_norm.reshape(all_dims),
            hat,
            rstd,
            block,
            grad_map,
            taps,
            pad_x,
            grads,
        )
        total = total.astype(F32).reshape(2, chans, hidden)
        grad_kernel = taps_total.reshape(ny * 8, 128)[:49, :panel].reshape(7, 7, panel)
        return output[None], grad_image[None], total[0], total[1].T, grad_kernel

    return shards


def solution(mesh):
    ny = 8
    nz = mesh.shape["sp"] // (2 * ny)
    return jax.shard_map(
        make_shards(ny, nz),
        mesh=mesh,
        in_specs=(
            P("sp", None, None, "ch"),
            P("sp", None, None, "ch"),
            P(None, None, "ch"),
            P(None, "ch"),
            P("ch", None),
        ),
        out_specs=(
            P("sp", None, None, "ch"),
            P("sp", None, None, "ch"),
            P(None, "ch"),
            P("ch", None),
            P(None, None, "ch"),
        ),
        check_vma=False,
    )
```

```python
import jax
import jax.numpy as jnp
from jax import lax
from jax.experimental import pallas as pl
from jax.experimental.pallas import tpu as pltpu
from jax.sharding import PartitionSpec as P

GRID_W = 8
MESH = pl.DeviceIdType.MESH
DIRS = ((-1, 0), (1, 0), (0, -1), (0, 1), (-1, -1), (-1, 1), (1, -1), (1, 1))
EDGE = 16
LEFT = 8
CHUNKS = 3
F32 = jnp.float32
BF16 = jnp.bfloat16


def greet(peers):
    barrier = pltpu.get_barrier_semaphore()
    for peer in peers:
        pl.semaphore_signal(barrier, inc=1, device_id=peer, device_id_type=MESH)
    pl.semaphore_wait(barrier, len(peers))


def send(src, dst, send_sem, recv_sem, peer):
    copy = pltpu.make_async_remote_copy(
        src_ref=src,
        dst_ref=dst,
        send_sem=send_sem,
        recv_sem=recv_sem,
        device_id=peer,
        device_id_type=MESH,
    )
    copy.start()
    return copy


def call(body, name, cid, out_shape, scratch):
    def run(*args):
        return pl.pallas_call(
            body,
            out_shape=out_shape,
            in_specs=[pl.BlockSpec(memory_space=pltpu.VMEM)] * len(args),
            out_specs=tuple([pl.BlockSpec(memory_space=pltpu.VMEM)] * len(out_shape)),
            scratch_shapes=scratch,
            compiler_params=pltpu.CompilerParams(
                collective_id=cid, has_side_effects=True, vmem_limit_bytes=20 * 2**20
            ),
            name=name,
        )(*args)

    return run


def shape(dims, dtype):
    return jax.ShapeDtypeStruct(dims, dtype)


def window(dr, dc, rows, cols):
    r = slice(0, rows) if dr == 0 else (slice(0, 3) if dr < 0 else slice(rows - 3, rows))
    c = slice(0, cols) if dc == 0 else (slice(0, EDGE) if dc < 0 else slice(cols - EDGE, cols))
    return r, c


def margin_peers():
    b, ch = lax.axis_index("sp"), lax.axis_index("ch")
    row, col = b // GRID_W, b % GRID_W
    peers = []
    for dr, dc in DIRS:
        r = lax.rem(row + dr + GRID_W, GRID_W)
        c = lax.rem(col + dc + GRID_W, GRID_W)
        peers.append((r * GRID_W + c, ch))
    return peers


def start_margins(block, lands, send_sem, recv_sem, peers):
    rows, cols = block.shape[0], block.shape[1]
    copies = []
    for k, (dr, dc) in enumerate(DIRS):
        r, c = window(dr, dc, rows, cols)
        copies.append(
            send(block.at[r, c], lands[k], send_sem.at[k], recv_sem.at[k], peers[k])
        )
    return copies


def fill_margins(pad, block, lands):
    b = lax.axis_index("sp")
    row, col = b // GRID_W, b % GRID_W
    rows, cols = block.shape[0], block.shape[1]
    pad[3 : 3 + rows, LEFT : LEFT + cols] = block[...].astype(F32)
    for k, (dr, dc) in enumerate(DIRS):
        keep = jnp.logical_and(
            jnp.logical_and(row - dr >= 0, row - dr < GRID_W),
            jnp.logical_and(col - dc >= 0, col - dc < GRID_W),
        )
        value = lands[k][...].astype(F32)
        value = value * jnp.where(keep, 1.0, 0.0).astype(F32)
        if dc:
            value = value[:, :3] if dc < 0 else value[:, EDGE - 3 :]
        top = 3 if dr == 0 else (0 if dr > 0 else 3 + rows)
        left = LEFT if dc == 0 else (LEFT - 3 if dc > 0 else LEFT + cols)
        pad[top : top + value.shape[0], left : left + value.shape[1]] = value


def ch_peers(n):
    b, me = lax.axis_index("sp"), lax.axis_index("ch")
    return me, [(b, lax.rem(me + d, n)) for d in range(1, n)]


def send_stats(stat, me, peers, first, second, send_sem, recv_sem):
    stat[me, 0:1, :] = first
    stat[me, 1:2, :] = second
    return [
        send(stat.at[me], stat.at[me], send_sem.at[d], recv_sem.at[d], peer)
        for d, peer in enumerate(peers)
    ]


def sum_stats(stat, copies):
    for copy in copies:
        copy.wait()
    total = stat[0]
    for k in range(1, stat.shape[0]):
        total = total + stat[k]
    return total[0:1], total[1:2]


def to_channels(wide, panel):
    return wide[...].T[0:panel]


def to_pixels(tall, value, dims):
    rows, cols, panel = dims
    tall[0:panel, :] = value
    turned = tall[...].T
    return [turned[p * cols : (p + 1) * cols, 0:panel] for p in range(rows)]


def front_kernel(*refs):
    block, taps, grad_map = refs[0:3]
    normed_all, grad_all, hat, rstd, pad = refs[3:8]
    lands, msem, mrsem = refs[8:16], refs[16], refs[17]
    wide, stat, ssem, rsem = refs[18:22]
    rows, cols, panel = block.shape
    n = normed_all.shape[0]
    chans = n * panel
    me, peers = ch_peers(n)
    near = margin_peers()
    stat[me] = jnp.zeros(stat.shape[1:], F32)
    wide[...] = jnp.zeros_like(wide)
    for p in range(rows):
        wide[p * cols : (p + 1) * cols, 0:panel] = grad_map[p].astype(F32)
    grad_all[me] = to_channels(wide, panel).astype(BF16)
    greet(near + peers)
    copies = start_margins(block, lands, msem, mrsem, near)
    grads = [
        send(grad_all.at[me], grad_all.at[me], ssem.at[1, d], rsem.at[1, d], peer)
        for d, peer in enumerate(peers)
    ]
    pad[...] = jnp.zeros_like(pad)
    for copy in copies:
        copy.wait()
    fill_margins(pad, block, lands)
    rows_f = [taps[i].astype(F32) for i in range(7)]
    for p in range(rows):
        total = jnp.zeros(block.shape[1:], F32)
        for i in range(7):
            for j in range(7):
                start = LEFT - 3 + j
                total = total + rows_f[i][j : j + 1] * pad[p + i, start : start + cols, :]
        wide[p * cols : (p + 1) * cols, 0:panel] = total.astype(BF16).astype(F32)
    value = to_channels(wide, panel)
    stats = send_stats(
        stat,
        me,
        peers,
        jnp.sum(value, axis=0, keepdims=True),
        jnp.sum(value * value, axis=0, keepdims=True),
        ssem.at[0],
        rsem.at[0],
    )
    first, second = sum_stats(stat, stats)
    mean = first / chans
    var = second / chans - mean * mean
    scale = lax.rsqrt(var + 1e-06)
    rstd[...] = scale
    local = (value - mean) * scale
    hat[...] = local
    normed_all[me] = local.astype(BF16)
    outs = [
        send(normed_all.at[me], normed_all.at[me], ssem.at[2, d], rsem.at[2, d], peer)
        for d, peer in enumerate(peers)
    ]
    for copy in grads + outs:
        copy.wait()


def back_kernel(*refs):
    part_out, part_norm, hat, rstd, image, grad_map, taps, pad_x, grads = refs[0:9]
    output, grad_image, out, taps_out = refs[9:13]
    lands, msem, mrsem = refs[13:21], refs[21], refs[22]
    land, stat, csem, crsem, tall, d_conv, pad, mytaps = refs[23:31]
    land0, mine, land1, land2, tland0, tmine, tland1, tland2, ssem, rsem = refs[31:41]
    ring_send, ring_recv, pair_send, pair_recv = refs[41:45]

    n, panel, pixels = part_out.shape
    rows, cols, _ = image.shape
    chans = n * panel
    b, ch = lax.axis_index("sp"), lax.axis_index("ch")
    me, peers = ch_peers(n)
    near = margin_peers()
    ny, nz = grads.shape[1], land2.shape[0]
    core, y, z = b % 2, (b // 2) % ny, b // (2 * ny)
    other = (b + 1 - 2 * core, ch)
    ys = [lax.rem(y + d, ny) for d in range(1, ny)]
    zs = [lax.rem(z + d, nz) for d in range(1, nz)]
    y_peers = [((z * ny + k) * 2 + core, ch) for k in ys]
    z_peers = [((k * ny + y) * 2 + core, ch) for k in zs]
    stat[me] = jnp.zeros(stat.shape[1:], F32)
    greet(peers + near + [other] + y_peers + z_peers)

    norms = [
        send(part_norm.at[peer[1]], land.at[0, d], csem.at[0, d], crsem.at[0, d], peer)
        for d, peer in enumerate(peers)
    ]
    outs = [
        send(part_out.at[peer[1]], land.at[1, d], csem.at[1, d], crsem.at[1, d], peer)
        for d, peer in enumerate(peers)
    ]
    order = ys + [y]
    firsts = [
        send(grads.at[1 - core, k], land0.at[k], ssem.at[0, d], rsem.at[0, d], other)
        for d, k in enumerate(order)
    ]
    tall[...] = jnp.zeros_like(tall)
    mytaps[...] = jnp.zeros_like(mytaps)
    pad[...] = jnp.zeros_like(pad)

    moves = []
    for d, k in enumerate(order):
        firsts[d].wait()
        mine[k] = (grads[core, k].astype(F32) + land0[k].astype(F32)).astype(BF16)
        if d < ny - 1:
            moves.append(
                send(mine.at[k], land1.at[d], ssem.at[2, d], rsem.at[2, d], y_peers[d])
            )

    d_norm = part_norm[me].astype(F32)
    for d, copy in enumerate(norms):
        copy.wait()
        d_norm = d_norm + land[0, d].astype(F32)
    local = hat[...]
    stats = send_stats(
        stat,
        me,
        peers,
        jnp.sum(d_norm, axis=0, keepdims=True),
        jnp.sum(d_norm * local, axis=0, keepdims=True),
        csem.at[2],
        crsem.at[2],
    )
    branch = part_out[me].astype(F32)
    for d, copy in enumerate(outs):
        copy.wait()
        branch = branch + land[1, d].astype(F32)
    for p, value in enumerate(to_pixels(tall, branch, image.shape)):
        output[p] = (image[p].astype(F32) + value).astype(BF16)
    first, second = sum_stats(stat, stats)
    back = rstd[...] * (d_norm - first / chans - local * second / chans)
    for p, value in enumerate(to_pixels(tall, back, image.shape)):
        d_conv[p] = value.astype(BF16)
    margins = start_margins(d_conv, lands, msem, mrsem, near)

    for i in range(7):
        for j in range(7):
            start = LEFT - 3 + j
            total = jnp.zeros(image.shape[1:], F32)
            for p in range(rows):
                total = total + d_conv[p].astype(F32) * pad_x[p + i, start : start + cols, :]
            mytaps[i, j : j + 1, 0:panel] = jnp.sum(total, axis=0, keepdims=True)
    tfirst = send(mytaps, tland0, ssem.at[1, 0], rsem.at[1, 0], other)

    total = mine[y].astype(F32)
    for d in range(ny - 1):
        moves[d].wait()
        total = total + land1[d].astype(F32)
    land2[z] = total.astype(BF16)
    moves = [
        send(land2.at[z], land2.at[z], ssem.at[4, d], rsem.at[4, d], z_peers[d])
        for d in range(nz - 1)
    ]

    tfirst.wait()
    tmine[...] = mytaps[...] + tland0[...]
    tmoves = [
        send(tmine.at[ys[d]], tland1.at[d], ssem.at[3, d], rsem.at[3, d], y_peers[d])
        for d in range(ny - 1)
    ]

    for copy in margins:
        copy.wait()
    fill_margins(pad, d_conv, lands)
    rows_f = [taps[i].astype(F32) for i in range(7)]
    for p in range(rows):
        total = grad_map[p].astype(F32)
        for i in range(7):
            for j in range(7):
                start = LEFT + 3 - j
                total = total + rows_f[i][j : j + 1] * pad[p + 6 - i, start : start + cols, :]
        grad_image[p] = total.astype(BF16)

    for copy in moves:
        copy.wait()
    total = land2[0].astype(F32)
    for k in range(1, nz):
        total = total + land2[k].astype(F32)
    out[core, y] = total.astype(BF16)
    size = out.shape[2] // CHUNKS
    ring = [((z * ny + k) * 2 + core, ch) for k in (lax.rem(y + 1, ny), lax.rem(y + ny - 1, ny))]

    def part(k, c):
        return out.at[core, k, c * size : (c + 1) * size]

    def pass_on(way, step, c, k):
        sems = ring_send.at[way, step, c], ring_recv.at[way, step, c]
        return send(part(k, c), part(k, c), *sems, ring[way])

    def share(step, c, k):
        return send(part(k, c), part(k, c), pair_send.at[step, c], pair_recv.at[step, c], other)

    def goes(way, step, c):
        return step < ny // 2 - 1 or (step == ny // 2 - 1 and c % 2 == way)

    flight = {
        (way, 0, c): pass_on(way, 0, c, y) for c in range(CHUNKS) for way in range(2)
    }
    pairs = [share(0, c, y) for c in range(CHUNKS)]

    ttotal = tmine[y]
    for d in range(ny - 1):
        tmoves[d].wait()
        ttotal = ttotal + tland1[d]
    tland2[z] = ttotal
    tmoves = [
        send(tland2.at[z], tland2.at[z], ssem.at[5, d], rsem.at[5, d], z_peers[d])
        for d in range(nz - 1)
    ]
    for copy in tmoves:
        copy.wait()
    ttotal = tland2[0]
    for k in range(1, nz):
        ttotal = ttotal + tland2[k]
    taps_out[y] = ttotal
    tmoves = [
        send(taps_out.at[y], taps_out.at[y], ssem.at[7, d], rsem.at[7, d], y_peers[d])
        for d in range(ny - 1)
    ]

    for step in range(ny // 2):
        for c in range(CHUNKS):
            for way in range(2):
                if not goes(way, step, c):
                    continue
                flight[way, step, c].wait()
                away = step + 1
                k = lax.rem(y + (ny - away if way == 0 else away), ny)
                if goes(way, away, c):
                    flight[way, away, c] = pass_on(way, away, c, k)
                pairs.append(share(away if way == 0 else ny - away, c, k))
    for copy in tmoves + pairs:
        copy.wait()


def make_shards(ny, nz):
    def shards(image, cotangent, kernel, w_in, w_out):
        block, grad_map = image[0], cotangent[0]
        rows, cols, panel = block.shape
        pixels = rows * cols
        n = w_in.shape[0] // panel
        hidden = w_in.shape[1]
        chans = w_in.shape[0]
        lands = []
        for dr, dc in DIRS:
            lands.append(
                pltpu.VMEM((3 if dr else rows, EDGE if dc else cols, panel), BF16)
            )

        def sems(*dims):
            return [pltpu.SemaphoreType.DMA(dims), pltpu.SemaphoreType.DMA(dims)]

        padded = (rows + 6, cols + 2 * LEFT, panel)
        all_dims = (n, panel, pixels)
        normed_t, gall_t, hat, rstd, pad_x = call(
            front_kernel,
            "front",
            1,
            (
                shape(all_dims, BF16),
                shape(all_dims, BF16),
                shape((panel, pixels), F32),
                shape((1, pixels), F32),
                shape(padded, F32),
            ),
            lands
            + sems(8)
            + [pltpu.VMEM((pixels, 128), F32), pltpu.VMEM((n, 8, pixels), F32)]
            + sems(3, n - 1),
        )(block, kernel, grad_map)
        normed_t = normed_t.reshape(chans, pixels)
        gall_t = gall_t.reshape(chans, pixels)

        def mm(a, b, dims):
            return lax.dot_general(a, b, (dims, ((), ())), preferred_element_type=F32)

        pre = mm(w_in, normed_t, ((0,), (0,)))
        half = 0.5 * (1.0 + jax.scipy.special.erf(pre / jnp.sqrt(2.0)))
        act = (pre * half).astype(BF16)
        slope = half + pre * jnp.exp(-0.5 * pre * pre) / jnp.sqrt(2.0 * jnp.pi)
        d_act = mm(w_out, gall_t, ((1,), (0,)))
        d_pre = (d_act * slope).astype(BF16)
        part_out = mm(w_out, act, ((0,), (0,))).astype(BF16)
        part_norm = mm(w_in, d_pre, ((1,), (0,))).astype(BF16)
        grad_in = mm(normed_t, d_pre, ((1,), (1,))).astype(BF16)
        grad_out = mm(act, gall_t, ((1,), (1,))).astype(BF16)

        piece = chans // ny
        grad_in = grad_in.reshape(ny, piece, hidden)
        halves = [
            grad_out[:, at : at + hidden].reshape(-1, piece, hidden)
            for at in range(0, chans, hidden)
        ]
        grads = jnp.concatenate([grad_in] + halves).reshape(2, ny, piece, hidden)
        tdims = (ny, 8, 128)
        output, grad_image, total, taps_total = call(
            back_kernel,
            "back",
            2,
            (
                shape(block.shape, BF16),
                shape(block.shape, BF16),
                shape(grads.shape, BF16),
                shape(tdims, F32),
            ),
            lands
            + sems(8)
            + [pltpu.VMEM((2, n - 1, panel, pixels), BF16), pltpu.VMEM((n, 8, pixels), F32)]
            + sems(3, n - 1)
            + [
                pltpu.VMEM((128, pixels), F32),
                pltpu.VMEM(block.shape, BF16),
                pltpu.VMEM(padded, F32),
                pltpu.VMEM(tdims, F32),
                pltpu.VMEM((ny, piece, hidden), BF16),
                pltpu.VMEM((ny, piece, hidden), BF16),
                pltpu.VMEM((ny - 1, piece, hidden), BF16),
                pltpu.VMEM((nz, piece, hidden), BF16),
                pltpu.VMEM(tdims, F32),
                pltpu.VMEM(tdims, F32),
                pltpu.VMEM((ny - 1, 8, 128), F32),
                pltpu.VMEM((nz, 8, 128), F32),
            ]
            + sems(9, ny)
            + sems(2, ny // 2, CHUNKS)
            + sems(ny, CHUNKS),
        )(
            part_out.reshape(all_dims),
            part_norm.reshape(all_dims),
            hat,
            rstd,
            block,
            grad_map,
            kernel,
            pad_x,
            grads,
        )
        total = total.astype(F32)
        grad_in = total[0].reshape(chans, hidden)
        down = hidden // piece
        grad_out = jnp.concatenate(
            [total[1, k : k + down].reshape(hidden, hidden) for k in range(0, ny, down)], axis=1
        )
        grad_kernel = taps_total[:7, :7, :panel]
        return output[None], grad_image[None], grad_in, grad_out, grad_kernel

    return shards


def solution(mesh):
    ny = 8
    nz = mesh.shape["sp"] // (2 * ny)
    return jax.shard_map(
        make_shards(ny, nz),
        mesh=mesh,
        in_specs=(
            P("sp", None, None, "ch"),
            P("sp", None, None, "ch"),
            P(None, None, "ch"),
            P(None, "ch"),
            P("ch", None),
        ),
        out_specs=(
            P("sp", None, None, "ch"),
            P("sp", None, None, "ch"),
            P(None, "ch"),
            P("ch", None),
            P(None, None, "ch"),
        ),
        check_vma=False,
    )
```

```python
import jax
import jax.numpy as jnp
from jax import lax
from jax.experimental import pallas as pl
from jax.experimental.pallas import tpu as pltpu
from jax.sharding import PartitionSpec as P

GRID_W = 8
MESH = pl.DeviceIdType.MESH
DIRS = ((-1, 0), (1, 0), (0, -1), (0, 1), (-1, -1), (-1, 1), (1, -1), (1, 1))
EDGE = 16
LEFT = 8
CHUNKS = 3
F32 = jnp.float32
BF16 = jnp.bfloat16


def greet(peers):
    barrier = pltpu.get_barrier_semaphore()
    for peer in peers:
        pl.semaphore_signal(barrier, inc=1, device_id=peer, device_id_type=MESH)
    pl.semaphore_wait(barrier, len(peers))


def send(src, dst, send_sem, recv_sem, peer):
    copy = pltpu.make_async_remote_copy(
        src_ref=src,
        dst_ref=dst,
        send_sem=send_sem,
        recv_sem=recv_sem,
        device_id=peer,
        device_id_type=MESH,
    )
    copy.start()
    return copy


def call(body, name, cid, out_shape, scratch):
    def run(*args):
        return pl.pallas_call(
            body,
            out_shape=out_shape,
            in_specs=[pl.BlockSpec(memory_space=pltpu.VMEM)] * len(args),
            out_specs=tuple([pl.BlockSpec(memory_space=pltpu.VMEM)] * len(out_shape)),
            scratch_shapes=scratch,
            compiler_params=pltpu.CompilerParams(
                collective_id=cid, has_side_effects=True, vmem_limit_bytes=20 * 2**20
            ),
            name=name,
        )(*args)

    return run


def shape(dims, dtype):
    return jax.ShapeDtypeStruct(dims, dtype)


def window(dr, dc, rows, cols):
    r = slice(0, rows) if dr == 0 else (slice(0, 3) if dr < 0 else slice(rows - 3, rows))
    c = slice(0, cols) if dc == 0 else (slice(0, EDGE) if dc < 0 else slice(cols - EDGE, cols))
    return r, c


def margin_peers():
    b, ch = lax.axis_index("sp"), lax.axis_index("ch")
    row, col = b // GRID_W, b % GRID_W
    peers = []
    for dr, dc in DIRS:
        r = lax.rem(row + dr + GRID_W, GRID_W)
        c = lax.rem(col + dc + GRID_W, GRID_W)
        peers.append((r * GRID_W + c, ch))
    return peers


def start_margins(block, lands, send_sem, recv_sem, peers):
    rows, cols = block.shape[0], block.shape[1]
    copies = []
    for k, (dr, dc) in enumerate(DIRS):
        r, c = window(dr, dc, rows, cols)
        copies.append(
            send(block.at[r, c], lands[k], send_sem.at[k], recv_sem.at[k], peers[k])
        )
    return copies


def fill_margins(pad, block, lands):
    b = lax.axis_index("sp")
    row, col = b // GRID_W, b % GRID_W
    rows, cols = block.shape[0], block.shape[1]
    pad[3 : 3 + rows, LEFT : LEFT + cols] = block[...].astype(F32)
    for k, (dr, dc) in enumerate(DIRS):
        keep = jnp.logical_and(
            jnp.logical_and(row - dr >= 0, row - dr < GRID_W),
            jnp.logical_and(col - dc >= 0, col - dc < GRID_W),
        )
        value = lands[k][...].astype(F32)
        value = value * jnp.where(keep, 1.0, 0.0).astype(F32)
        if dc:
            value = value[:, :3] if dc < 0 else value[:, EDGE - 3 :]
        top = 3 if dr == 0 else (0 if dr > 0 else 3 + rows)
        left = LEFT if dc == 0 else (LEFT - 3 if dc > 0 else LEFT + cols)
        pad[top : top + value.shape[0], left : left + value.shape[1]] = value


def ch_peers(n):
    b, me = lax.axis_index("sp"), lax.axis_index("ch")
    return me, [(b, lax.rem(me + d, n)) for d in range(1, n)]


def send_stats(stat, me, peers, first, second, send_sem, recv_sem):
    stat[me, 0:1, :] = first
    stat[me, 1:2, :] = second
    return [
        send(stat.at[me], stat.at[me], send_sem.at[d], recv_sem.at[d], peer)
        for d, peer in enumerate(peers)
    ]


def sum_stats(stat, copies):
    for copy in copies:
        copy.wait()
    total = stat[0]
    for k in range(1, stat.shape[0]):
        total = total + stat[k]
    return total[0:1], total[1:2]


def to_channels(wide, panel):
    return wide[...].T[0:panel]


def to_pixels(tall, value, dims):
    rows, cols, panel = dims
    tall[0:panel, :] = value
    turned = tall[...].T
    return [turned[p * cols : (p + 1) * cols, 0:panel] for p in range(rows)]


def front_kernel(*refs):
    block, taps, grad_map = refs[0:3]
    normed_all, grad_all, hat, rstd, pad = refs[3:8]
    lands, msem, mrsem = refs[8:16], refs[16], refs[17]
    wide, stat, ssem, rsem = refs[18:22]
    rows, cols, panel = block.shape
    n = normed_all.shape[0]
    chans = n * panel
    me, peers = ch_peers(n)
    near = margin_peers()
    stat[me] = jnp.zeros(stat.shape[1:], F32)
    wide[...] = jnp.zeros_like(wide)
    for p in range(rows):
        wide[p * cols : (p + 1) * cols, 0:panel] = grad_map[p].astype(F32)
    grad_all[me] = to_channels(wide, panel).astype(BF16)
    greet(near + peers)
    copies = start_margins(block, lands, msem, mrsem, near)
    grads = [
        send(grad_all.at[me], grad_all.at[me], ssem.at[1, d], rsem.at[1, d], peer)
        for d, peer in enumerate(peers)
    ]
    pad[...] = jnp.zeros_like(pad)
    for copy in copies:
        copy.wait()
    fill_margins(pad, block, lands)
    rows_f = [taps[i].astype(F32) for i in range(7)]
    for p in range(rows):
        total = jnp.zeros(block.shape[1:], F32)
        for i in range(7):
            for j in range(7):
                start = LEFT - 3 + j
                total = total + rows_f[i][j : j + 1] * pad[p + i, start : start + cols, :]
        wide[p * cols : (p + 1) * cols, 0:panel] = total.astype(BF16).astype(F32)
    value = to_channels(wide, panel)
    stats = send_stats(
        stat,
        me,
        peers,
        jnp.sum(value, axis=0, keepdims=True),
        jnp.sum(value * value, axis=0, keepdims=True),
        ssem.at[0],
        rsem.at[0],
    )
    first, second = sum_stats(stat, stats)
    mean = first / chans
    var = second / chans - mean * mean
    scale = lax.rsqrt(var + 1e-06)
    rstd[...] = scale
    local = (value - mean) * scale
    hat[...] = local
    normed_all[me] = local.astype(BF16)
    outs = [
        send(normed_all.at[me], normed_all.at[me], ssem.at[2, d], rsem.at[2, d], peer)
        for d, peer in enumerate(peers)
    ]
    for copy in grads + outs:
        copy.wait()


def back_kernel(*refs):
    part_out, part_norm, hat, rstd, image, grad_map, taps, pad_x, grads = refs[0:9]
    output, grad_image, out, taps_out = refs[9:13]
    lands, msem, mrsem = refs[13:21], refs[21], refs[22]
    land, stat, csem, crsem, tall, d_conv, pad, mytaps = refs[23:31]
    land0, mine, land1, land2, tland0, tmine, tland1, tland2, ssem, rsem = refs[31:41]
    ring_send, ring_recv, pair_send, pair_recv = refs[41:45]
    sum_send, sum_recv, across_send, across_recv = refs[45:49]

    n, panel, pixels = part_out.shape
    rows, cols, _ = image.shape
    chans = n * panel
    b, ch = lax.axis_index("sp"), lax.axis_index("ch")
    me, peers = ch_peers(n)
    near = margin_peers()
    ny, nz = grads.shape[1], land2.shape[0]
    core, y, z = b % 2, (b // 2) % ny, b // (2 * ny)
    other = (b + 1 - 2 * core, ch)
    ys = [lax.rem(y + d, ny) for d in range(1, ny)]
    zs = [lax.rem(z + d, nz) for d in range(1, nz)]
    y_peers = [((z * ny + k) * 2 + core, ch) for k in ys]
    z_peers = [((k * ny + y) * 2 + core, ch) for k in zs]
    stat[me] = jnp.zeros(stat.shape[1:], F32)
    greet(peers + near + [other] + y_peers + z_peers)

    norms = [
        send(part_norm.at[peer[1]], land.at[0, d], csem.at[0, d], crsem.at[0, d], peer)
        for d, peer in enumerate(peers)
    ]
    outs = [
        send(part_out.at[peer[1]], land.at[1, d], csem.at[1, d], crsem.at[1, d], peer)
        for d, peer in enumerate(peers)
    ]
    half = ny // 2
    away = [half] + [a for d in range(half - 1, 0, -1) for a in (d, ny - d)] + [0]
    order = [lax.rem(y + a, ny) for a in away]
    firsts = [
        send(grads.at[1 - core, k], land0.at[k], ssem.at[0, d], rsem.at[0, d], other)
        for d, k in enumerate(order)
    ]
    tall[...] = jnp.zeros_like(tall)
    mytaps[...] = jnp.zeros_like(mytaps)
    pad[...] = jnp.zeros_like(pad)

    size = out.shape[2] // CHUNKS
    ring = [((z * ny + k) * 2 + core, ch) for k in (lax.rem(y + 1, ny), lax.rem(y + ny - 1, ny))]
    for d, k in enumerate(order):
        firsts[d].wait()
        mine[k] = (grads[core, k].astype(F32) + land0[k].astype(F32)).astype(BF16)
    sums, moves = {}, []
    for step in range(half + 1):
        for c in range(CHUNKS):
            part_rows = slice(c * size, (c + 1) * size)
            for way in range(2):
                reach = half if c % 2 == way else half - 1
                left = reach - step
                if left < 0:
                    continue
                k = lax.rem(y + (left if way == 0 else ny - left), ny)
                src = mine.at[k, part_rows]
                if step:
                    sums[way, step - 1, c].wait()
                    src = land1.at[way, step - 1, part_rows]
                if left and step:
                    src[...] = (src[...].astype(F32) + mine[k, part_rows].astype(F32)).astype(BF16)
                if left:
                    sums[way, step, c] = send(
                        src,
                        land1.at[way, step, part_rows],
                        sum_send.at[way, step, c],
                        sum_recv.at[way, step, c],
                        ring[way],
                    )
            if step == half:
                total = mine[y, part_rows].astype(F32)
                for way in range(2):
                    last = (half if c % 2 == way else half - 1) - 1
                    total = total + land1[way, last, part_rows].astype(F32)
                land2[z, part_rows] = total.astype(BF16)
                moves.append(
                    [
                        send(
                            land2.at[z, part_rows],
                            land2.at[z, part_rows],
                            across_send.at[c, d],
                            across_recv.at[c, d],
                            z_peers[d],
                        )
                        for d in range(nz - 1)
                    ]
                )

    d_norm = part_norm[me].astype(F32)
    for d, copy in enumerate(norms):
        copy.wait()
        d_norm = d_norm + land[0, d].astype(F32)
    local = hat[...]
    stats = send_stats(
        stat,
        me,
        peers,
        jnp.sum(d_norm, axis=0, keepdims=True),
        jnp.sum(d_norm * local, axis=0, keepdims=True),
        csem.at[2],
        crsem.at[2],
    )
    branch = part_out[me].astype(F32)
    for d, copy in enumerate(outs):
        copy.wait()
        branch = branch + land[1, d].astype(F32)
    for p, value in enumerate(to_pixels(tall, branch, image.shape)):
        output[p] = (image[p].astype(F32) + value).astype(BF16)
    first, second = sum_stats(stat, stats)
    back = rstd[...] * (d_norm - first / chans - local * second / chans)
    for p, value in enumerate(to_pixels(tall, back, image.shape)):
        d_conv[p] = value.astype(BF16)
    margins = start_margins(d_conv, lands, msem, mrsem, near)

    for i in range(7):
        for j in range(7):
            start = LEFT - 3 + j
            total = jnp.zeros(image.shape[1:], F32)
            for p in range(rows):
                total = total + d_conv[p].astype(F32) * pad_x[p + i, start : start + cols, :]
            mytaps[i, j : j + 1, 0:panel] = jnp.sum(total, axis=0, keepdims=True)
    tfirst = send(mytaps, tland0, ssem.at[1, 0], rsem.at[1, 0], other)

    def part(k, c):
        return out.at[core, k, c * size : (c + 1) * size]

    def pass_on(way, step, c, k):
        sems = ring_send.at[way, step, c], ring_recv.at[way, step, c]
        return send(part(k, c), part(k, c), *sems, ring[way])

    def share(step, c, k):
        return send(part(k, c), part(k, c), pair_send.at[step, c], pair_recv.at[step, c], other)

    def goes(way, step, c):
        return step < ny // 2 - 1 or (step == ny // 2 - 1 and c % 2 == way)

    flight, pairs = {}, []
    for c in range(CHUNKS):
        part_rows = slice(c * size, (c + 1) * size)
        for copy in moves[c]:
            copy.wait()
        total = land2[0, part_rows].astype(F32)
        for k in range(1, nz):
            total = total + land2[k, part_rows].astype(F32)
        out[core, y, part_rows] = total.astype(BF16)
        for way in range(2):
            flight[way, 0, c] = pass_on(way, 0, c, y)
        pairs.append(share(0, c, y))

    tfirst.wait()
    tmine[...] = mytaps[...] + tland0[...]
    tmoves = [
        send(tmine.at[ys[d]], tland1.at[d], ssem.at[3, d], rsem.at[3, d], y_peers[d])
        for d in range(ny - 1)
    ]

    for step in range(ny // 2):
        for c in range(CHUNKS):
            for way in range(2):
                if not goes(way, step, c):
                    continue
                flight[way, step, c].wait()
                away = step + 1
                k = lax.rem(y + (ny - away if way == 0 else away), ny)
                if goes(way, away, c):
                    flight[way, away, c] = pass_on(way, away, c, k)
                pairs.append(share(away if way == 0 else ny - away, c, k))
        if step == 0:
            ttotal = tmine[y]
            for d in range(ny - 1):
                tmoves[d].wait()
                ttotal = ttotal + tland1[d]
            tland2[z] = ttotal
            tmoves = [
                send(tland2.at[z], tland2.at[z], ssem.at[5, d], rsem.at[5, d], z_peers[d])
                for d in range(nz - 1)
            ]
        if step == 2:
            for copy in tmoves:
                copy.wait()
            ttotal = tland2[0]
            for k in range(1, nz):
                ttotal = ttotal + tland2[k]
            taps_out[y] = ttotal
            tmoves = [
                send(taps_out.at[y], taps_out.at[y], ssem.at[7, d], rsem.at[7, d], y_peers[d])
                for d in range(ny - 1)
            ]
    for copy in margins:
        copy.wait()
    fill_margins(pad, d_conv, lands)
    rows_f = [taps[i].astype(F32) for i in range(7)]
    for p in range(rows):
        total = grad_map[p].astype(F32)
        for i in range(7):
            for j in range(7):
                start = LEFT + 3 - j
                total = total + rows_f[i][j : j + 1] * pad[p + 6 - i, start : start + cols, :]
        grad_image[p] = total.astype(BF16)

    for copy in tmoves + pairs:
        copy.wait()


def make_shards(ny, nz):
    def shards(image, cotangent, kernel, w_in, w_out):
        block, grad_map = image[0], cotangent[0]
        rows, cols, panel = block.shape
        pixels = rows * cols
        n = w_in.shape[0] // panel
        hidden = w_in.shape[1]
        chans = w_in.shape[0]
        lands = []
        for dr, dc in DIRS:
            lands.append(
                pltpu.VMEM((3 if dr else rows, EDGE if dc else cols, panel), BF16)
            )

        def sems(*dims):
            return [pltpu.SemaphoreType.DMA(dims), pltpu.SemaphoreType.DMA(dims)]

        padded = (rows + 6, cols + 2 * LEFT, panel)
        all_dims = (n, panel, pixels)
        normed_t, gall_t, hat, rstd, pad_x = call(
            front_kernel,
            "front",
            1,
            (
                shape(all_dims, BF16),
                shape(all_dims, BF16),
                shape((panel, pixels), F32),
                shape((1, pixels), F32),
                shape(padded, F32),
            ),
            lands
            + sems(8)
            + [pltpu.VMEM((pixels, 128), F32), pltpu.VMEM((n, 8, pixels), F32)]
            + sems(3, n - 1),
        )(block, kernel, grad_map)
        normed_t = normed_t.reshape(chans, pixels)
        gall_t = gall_t.reshape(chans, pixels)

        def mm(a, b, dims):
            return lax.dot_general(a, b, (dims, ((), ())), preferred_element_type=F32)

        pre = mm(w_in, normed_t, ((0,), (0,)))
        half = 0.5 * (1.0 + jax.scipy.special.erf(pre / jnp.sqrt(2.0)))
        act = (pre * half).astype(BF16)
        slope = half + pre * jnp.exp(-0.5 * pre * pre) / jnp.sqrt(2.0 * jnp.pi)
        d_act = mm(w_out, gall_t, ((1,), (0,)))
        d_pre = (d_act * slope).astype(BF16)
        part_out = mm(w_out, act, ((0,), (0,))).astype(BF16)
        part_norm = mm(w_in, d_pre, ((1,), (0,))).astype(BF16)
        grad_in = mm(normed_t, d_pre, ((1,), (1,))).astype(BF16)
        grad_out = mm(act, gall_t, ((1,), (1,))).astype(BF16)

        piece = chans // ny
        grad_in = grad_in.reshape(ny, piece, hidden)
        halves = [
            grad_out[:, at : at + hidden].reshape(-1, piece, hidden)
            for at in range(0, chans, hidden)
        ]
        grads = jnp.concatenate([grad_in] + halves).reshape(2, ny, piece, hidden)
        tdims = (ny, 8, 128)
        output, grad_image, total, taps_total = call(
            back_kernel,
            "back",
            2,
            (
                shape(block.shape, BF16),
                shape(block.shape, BF16),
                shape(grads.shape, BF16),
                shape(tdims, F32),
            ),
            lands
            + sems(8)
            + [pltpu.VMEM((2, n - 1, panel, pixels), BF16), pltpu.VMEM((n, 8, pixels), F32)]
            + sems(3, n - 1)
            + [
                pltpu.VMEM((128, pixels), F32),
                pltpu.VMEM(block.shape, BF16),
                pltpu.VMEM(padded, F32),
                pltpu.VMEM(tdims, F32),
                pltpu.VMEM((ny, piece, hidden), BF16),
                pltpu.VMEM((ny, piece, hidden), BF16),
                pltpu.VMEM((2, ny // 2, piece, hidden), BF16),
                pltpu.VMEM((nz, piece, hidden), BF16),
                pltpu.VMEM(tdims, F32),
                pltpu.VMEM(tdims, F32),
                pltpu.VMEM((ny - 1, 8, 128), F32),
                pltpu.VMEM((nz, 8, 128), F32),
            ]
            + sems(9, ny)
            + sems(2, ny // 2, CHUNKS)
            + sems(ny, CHUNKS)
            + sems(2, ny // 2, CHUNKS)
            + sems(CHUNKS, nz - 1),
        )(
            part_out.reshape(all_dims),
            part_norm.reshape(all_dims),
            hat,
            rstd,
            block,
            grad_map,
            kernel,
            pad_x,
            grads,
        )
        total = total.astype(F32)
        grad_in = total[0].reshape(chans, hidden)
        down = hidden // piece
        grad_out = jnp.concatenate(
            [total[1, k : k + down].reshape(hidden, hidden) for k in range(0, ny, down)], axis=1
        )
        grad_kernel = taps_total[:7, :7, :panel]
        return output[None], grad_image[None], grad_in, grad_out, grad_kernel

    return shards


def solution(mesh):
    ny = 8
    nz = mesh.shape["sp"] // (2 * ny)
    return jax.shard_map(
        make_shards(ny, nz),
        mesh=mesh,
        in_specs=(
            P("sp", None, None, "ch"),
            P("sp", None, None, "ch"),
            P(None, None, "ch"),
            P(None, "ch"),
            P("ch", None),
        ),
        out_specs=(
            P("sp", None, None, "ch"),
            P("sp", None, None, "ch"),
            P(None, "ch"),
            P("ch", None),
            P(None, None, "ch"),
        ),
        check_vma=False,
    )
```

```python
import jax
import jax.numpy as jnp
from jax import lax
from jax.experimental import pallas as pl
from jax.experimental.pallas import tpu as pltpu
from jax.sharding import PartitionSpec as P

GRID_W = 8
MESH = pl.DeviceIdType.MESH
DIRS = ((-1, 0), (1, 0), (0, -1), (0, 1), (-1, -1), (-1, 1), (1, -1), (1, 1))
EDGE = 16
LEFT = 8
CHUNKS = 3
F32 = jnp.float32
BF16 = jnp.bfloat16


def mm(a, b, dims):
    return lax.dot_general(a, b, (dims, ((), ())), preferred_element_type=F32)


def greet(peers, between=None):
    barrier = pltpu.get_barrier_semaphore()
    for peer in peers:
        pl.semaphore_signal(barrier, inc=1, device_id=peer, device_id_type=MESH)
    if between is not None:
        between()
    pl.semaphore_wait(barrier, len(peers))


def send(src, dst, send_sem, recv_sem, peer):
    copy = pltpu.make_async_remote_copy(
        src_ref=src,
        dst_ref=dst,
        send_sem=send_sem,
        recv_sem=recv_sem,
        device_id=peer,
        device_id_type=MESH,
    )
    copy.start()
    return copy


def call(body, name, cid, out_shape, scratch):
    def run(*args):
        return pl.pallas_call(
            body,
            out_shape=out_shape,
            in_specs=[pl.BlockSpec(memory_space=pltpu.VMEM)] * len(args),
            out_specs=tuple([pl.BlockSpec(memory_space=pltpu.VMEM)] * len(out_shape)),
            scratch_shapes=scratch,
            compiler_params=pltpu.CompilerParams(
                collective_id=cid, has_side_effects=True, vmem_limit_bytes=20 * 2**20
            ),
            name=name,
        )(*args)

    return run


def shape(dims, dtype):
    return jax.ShapeDtypeStruct(dims, dtype)


def window(dr, dc, rows, cols):
    r = slice(0, rows) if dr == 0 else (slice(0, 3) if dr < 0 else slice(rows - 3, rows))
    c = slice(0, cols) if dc == 0 else (slice(0, EDGE) if dc < 0 else slice(cols - EDGE, cols))
    return r, c


def margin_peers():
    b, ch = lax.axis_index("sp"), lax.axis_index("ch")
    row, col = b // GRID_W, b % GRID_W
    peers = []
    for dr, dc in DIRS:
        r = lax.rem(row + dr + GRID_W, GRID_W)
        c = lax.rem(col + dc + GRID_W, GRID_W)
        peers.append((r * GRID_W + c, ch))
    return peers


def start_margins(block, lands, send_sem, recv_sem, peers):
    rows, cols = block.shape[0], block.shape[1]
    copies = []
    for k, (dr, dc) in enumerate(DIRS):
        r, c = window(dr, dc, rows, cols)
        copies.append(
            send(block.at[r, c], lands[k], send_sem.at[k], recv_sem.at[k], peers[k])
        )
    return copies


def fill_margins(pad, block, lands):
    b = lax.axis_index("sp")
    row, col = b // GRID_W, b % GRID_W
    rows, cols = block.shape[0], block.shape[1]
    pad[3 : 3 + rows, LEFT : LEFT + cols] = block[...].astype(F32)
    for k, (dr, dc) in enumerate(DIRS):
        keep = jnp.logical_and(
            jnp.logical_and(row - dr >= 0, row - dr < GRID_W),
            jnp.logical_and(col - dc >= 0, col - dc < GRID_W),
        )
        value = lands[k][...].astype(F32)
        value = value * jnp.where(keep, 1.0, 0.0).astype(F32)
        if dc:
            value = value[:, :3] if dc < 0 else value[:, EDGE - 3 :]
        top = 3 if dr == 0 else (0 if dr > 0 else 3 + rows)
        left = LEFT if dc == 0 else (LEFT - 3 if dc > 0 else LEFT + cols)
        pad[top : top + value.shape[0], left : left + value.shape[1]] = value


def ch_peers(n):
    b, me = lax.axis_index("sp"), lax.axis_index("ch")
    return me, [(b, lax.rem(me + d, n)) for d in range(1, n)]


def send_stats(stat, me, peers, first, second, send_sem, recv_sem):
    stat[me, 0:1, :] = first
    stat[me, 1:2, :] = second
    return [
        send(stat.at[me], stat.at[me], send_sem.at[d], recv_sem.at[d], peer)
        for d, peer in enumerate(peers)
    ]


def sum_stats(stat, copies):
    for copy in copies:
        copy.wait()
    total = stat[0]
    for k in range(1, stat.shape[0]):
        total = total + stat[k]
    return total[0:1], total[1:2]


def to_channels(wide, panel):
    return wide[...].T[0:panel]


def to_pixels(tall, value, dims):
    rows, cols, panel = dims
    tall[0:panel, :] = value
    turned = tall[...].T
    return [turned[p * cols : (p + 1) * cols, 0:panel] for p in range(rows)]


def front_kernel(*refs):
    block, taps, grad_map = refs[0:3]
    normed_all, grad_all, hat, rstd, pad = refs[3:8]
    lands, msem, mrsem = refs[8:16], refs[16], refs[17]
    wide, stat, ssem, rsem = refs[18:22]
    rows, cols, panel = block.shape
    n = normed_all.shape[0]
    chans = n * panel
    me, peers = ch_peers(n)
    near = margin_peers()
    stat[me] = jnp.zeros(stat.shape[1:], F32)
    wide[...] = jnp.zeros_like(wide)
    for p in range(rows):
        wide[p * cols : (p + 1) * cols, 0:panel] = grad_map[p].astype(F32)
    grad_all[me] = to_channels(wide, panel).astype(BF16)
    greet(near + peers)
    copies = start_margins(block, lands, msem, mrsem, near)
    grads = [
        send(grad_all.at[me], grad_all.at[me], ssem.at[1, d], rsem.at[1, d], peer)
        for d, peer in enumerate(peers)
    ]
    pad[...] = jnp.zeros_like(pad)
    for copy in copies:
        copy.wait()
    fill_margins(pad, block, lands)
    rows_f = [taps[i].astype(F32) for i in range(7)]
    for p in range(rows):
        total = jnp.zeros(block.shape[1:], F32)
        for i in range(7):
            for j in range(7):
                start = LEFT - 3 + j
                total = total + rows_f[i][j : j + 1] * pad[p + i, start : start + cols, :]
        wide[p * cols : (p + 1) * cols, 0:panel] = total.astype(BF16).astype(F32)
    value = to_channels(wide, panel)
    stats = send_stats(
        stat,
        me,
        peers,
        jnp.sum(value, axis=0, keepdims=True),
        jnp.sum(value * value, axis=0, keepdims=True),
        ssem.at[0],
        rsem.at[0],
    )
    first, second = sum_stats(stat, stats)
    mean = first / chans
    var = second / chans - mean * mean
    scale = lax.rsqrt(var + 1e-06)
    rstd[...] = scale
    local = (value - mean) * scale
    hat[...] = local
    normed_all[me] = local.astype(BF16)
    outs = [
        send(normed_all.at[me], normed_all.at[me], ssem.at[2, d], rsem.at[2, d], peer)
        for d, peer in enumerate(peers)
    ]
    for copy in grads + outs:
        copy.wait()


def back_kernel(*refs):
    w_in, w_out, act, d_pre, normed_all, grad_all = refs[0:6]
    part_out, part_norm, grads = refs[52:55]
    hat, rstd, image, grad_map, taps, pad_x = refs[6:12]
    refs = refs[3:]
    output, grad_image, out, taps_out = refs[9:13]
    lands, msem, mrsem = refs[13:21], refs[21], refs[22]
    land, stat, csem, crsem, tall, d_conv, pad, mytaps = refs[23:31]
    land0, mine, land1, land2, tland0, tmine, tland1, tland2, ssem, rsem = refs[31:41]
    ring_send, ring_recv, pair_send, pair_recv = refs[41:45]
    sum_send, sum_recv, across_send, across_recv = refs[45:49]

    n, panel, pixels = part_out.shape
    rows, cols, _ = image.shape
    chans = n * panel
    b, ch = lax.axis_index("sp"), lax.axis_index("ch")
    me, peers = ch_peers(n)
    near = margin_peers()
    ny, nz = grads.shape[1], land2.shape[0]
    core, y, z = b % 2, (b // 2) % ny, b // (2 * ny)
    other = (b + 1 - 2 * core, ch)
    ys = [lax.rem(y + d, ny) for d in range(1, ny)]
    zs = [lax.rem(z + d, nz) for d in range(1, nz)]
    y_peers = [((z * ny + k) * 2 + core, ch) for k in ys]
    z_peers = [((k * ny + y) * 2 + core, ch) for k in zs]
    stat[me] = jnp.zeros(stat.shape[1:], F32)

    def first_products():
        part_norm[...] = (
            mm(w_in[...], d_pre[...], ((1,), (0,))).astype(BF16).reshape(part_norm.shape)
        )
        normed = normed_all[...].reshape(chans, pixels)
        grad_in = mm(normed, d_pre[...], ((1,), (1,))).astype(BF16)
        grads[0] = grad_in.reshape(grads.shape[1:])

    greet(peers + near + [other] + y_peers + z_peers, first_products)

    norms = [
        send(part_norm.at[peer[1]], land.at[0, d], csem.at[0, d], crsem.at[0, d], peer)
        for d, peer in enumerate(peers)
    ]
    hidden = act.shape[0]
    down = hidden // panel
    for k in range(0, n, down):
        panels = grad_all[k : k + down].reshape(hidden, pixels)
        grad_out = mm(act[...], panels, ((1,), (1,))).astype(BF16)
        grads[1, k : k + down] = grad_out.reshape(down, panel, hidden)
    half = ny // 2
    away = [half] + [a for d in range(half - 1, 0, -1) for a in (d, ny - d)] + [0]
    order = [lax.rem(y + a, ny) for a in away]
    firsts = [
        send(grads.at[1 - core, k], land0.at[k], ssem.at[0, d], rsem.at[0, d], other)
        for d, k in enumerate(order)
    ]
    part_out[...] = (
        mm(w_out[...], act[...], ((0,), (0,))).astype(BF16).reshape(part_out.shape)
    )
    outs = [
        send(part_out.at[peer[1]], land.at[1, d], csem.at[1, d], crsem.at[1, d], peer)
        for d, peer in enumerate(peers)
    ]
    tall[...] = jnp.zeros_like(tall)
    mytaps[...] = jnp.zeros_like(mytaps)
    pad[...] = jnp.zeros_like(pad)

    size = out.shape[2] // CHUNKS
    ring = [((z * ny + k) * 2 + core, ch) for k in (lax.rem(y + 1, ny), lax.rem(y + ny - 1, ny))]
    for d, k in enumerate(order):
        firsts[d].wait()
        mine[k] = (grads[core, k].astype(F32) + land0[k].astype(F32)).astype(BF16)
    sums, moves = {}, []
    for step in range(half + 1):
        for c in range(CHUNKS):
            part_rows = slice(c * size, (c + 1) * size)
            for way in range(2):
                reach = half if c % 2 == way else half - 1
                left = reach - step
                if left < 0:
                    continue
                k = lax.rem(y + (left if way == 0 else ny - left), ny)
                src = mine.at[k, part_rows]
                if step:
                    sums[way, step - 1, c].wait()
                    src = land1.at[way, step - 1, part_rows]
                if left and step:
                    src[...] = (src[...].astype(F32) + mine[k, part_rows].astype(F32)).astype(BF16)
                if left:
                    sums[way, step, c] = send(
                        src,
                        land1.at[way, step, part_rows],
                        sum_send.at[way, step, c],
                        sum_recv.at[way, step, c],
                        ring[way],
                    )
            if step == half:
                total = mine[y, part_rows].astype(F32)
                for way in range(2):
                    last = (half if c % 2 == way else half - 1) - 1
                    total = total + land1[way, last, part_rows].astype(F32)
                land2[z, part_rows] = total.astype(BF16)
                moves.append(
                    [
                        send(
                            land2.at[z, part_rows],
                            land2.at[z, part_rows],
                            across_send.at[c, d],
                            across_recv.at[c, d],
                            z_peers[d],
                        )
                        for d in range(nz - 1)
                    ]
                )

    d_norm = part_norm[me].astype(F32)
    for d, copy in enumerate(norms):
        copy.wait()
        d_norm = d_norm + land[0, d].astype(F32)
    local = hat[...]
    stats = send_stats(
        stat,
        me,
        peers,
        jnp.sum(d_norm, axis=0, keepdims=True),
        jnp.sum(d_norm * local, axis=0, keepdims=True),
        csem.at[2],
        crsem.at[2],
    )
    branch = part_out[me].astype(F32)
    for d, copy in enumerate(outs):
        copy.wait()
        branch = branch + land[1, d].astype(F32)
    for p, value in enumerate(to_pixels(tall, branch, image.shape)):
        output[p] = (image[p].astype(F32) + value).astype(BF16)
    first, second = sum_stats(stat, stats)
    back = rstd[...] * (d_norm - first / chans - local * second / chans)
    for p, value in enumerate(to_pixels(tall, back, image.shape)):
        d_conv[p] = value.astype(BF16)
    margins = start_margins(d_conv, lands, msem, mrsem, near)

    for i in range(7):
        for j in range(7):
            start = LEFT - 3 + j
            total = jnp.zeros(image.shape[1:], F32)
            for p in range(rows):
                total = total + d_conv[p].astype(F32) * pad_x[p + i, start : start + cols, :]
            mytaps[i, j : j + 1, 0:panel] = jnp.sum(total, axis=0, keepdims=True)
    tfirst = send(mytaps, tland0, ssem.at[1, 0], rsem.at[1, 0], other)

    def part(k, c):
        return out.at[core, k, c * size : (c + 1) * size]

    def pass_on(way, step, c, k):
        sems = ring_send.at[way, step, c], ring_recv.at[way, step, c]
        return send(part(k, c), part(k, c), *sems, ring[way])

    def share(step, c, k):
        return send(part(k, c), part(k, c), pair_send.at[step, c], pair_recv.at[step, c], other)

    def goes(way, step, c):
        return step < ny // 2 - 1 or (step == ny // 2 - 1 and c % 2 == way)

    flight, pairs = {}, []
    for c in range(CHUNKS):
        part_rows = slice(c * size, (c + 1) * size)
        for copy in moves[c]:
            copy.wait()
        total = land2[0, part_rows].astype(F32)
        for k in range(1, nz):
            total = total + land2[k, part_rows].astype(F32)
        out[core, y, part_rows] = total.astype(BF16)
        for way in range(2):
            flight[way, 0, c] = pass_on(way, 0, c, y)
        pairs.append(share(0, c, y))

    tfirst.wait()
    tmine[...] = mytaps[...] + tland0[...]
    tmoves = [
        send(tmine.at[ys[d]], tland1.at[d], ssem.at[3, d], rsem.at[3, d], y_peers[d])
        for d in range(ny - 1)
    ]

    for step in range(ny // 2):
        for c in range(CHUNKS):
            for way in range(2):
                if not goes(way, step, c):
                    continue
                flight[way, step, c].wait()
                away = step + 1
                k = lax.rem(y + (ny - away if way == 0 else away), ny)
                if goes(way, away, c):
                    flight[way, away, c] = pass_on(way, away, c, k)
                pairs.append(share(away if way == 0 else ny - away, c, k))
        if step == 0:
            ttotal = tmine[y]
            for d in range(ny - 1):
                tmoves[d].wait()
                ttotal = ttotal + tland1[d]
            tland2[z] = ttotal
            tmoves = [
                send(tland2.at[z], tland2.at[z], ssem.at[5, d], rsem.at[5, d], z_peers[d])
                for d in range(nz - 1)
            ]
        if step == 2:
            for copy in tmoves:
                copy.wait()
            ttotal = tland2[0]
            for k in range(1, nz):
                ttotal = ttotal + tland2[k]
            taps_out[y] = ttotal
            tmoves = [
                send(taps_out.at[y], taps_out.at[y], ssem.at[7, d], rsem.at[7, d], y_peers[d])
                for d in range(ny - 1)
            ]
    for copy in margins:
        copy.wait()
    fill_margins(pad, d_conv, lands)
    rows_f = [taps[i].astype(F32) for i in range(7)]
    for p in range(rows):
        total = grad_map[p].astype(F32)
        for i in range(7):
            for j in range(7):
                start = LEFT + 3 - j
                total = total + rows_f[i][j : j + 1] * pad[p + 6 - i, start : start + cols, :]
        grad_image[p] = total.astype(BF16)

    for copy in tmoves + pairs:
        copy.wait()


def make_shards(ny, nz):
    def shards(image, cotangent, kernel, w_in, w_out):
        block, grad_map = image[0], cotangent[0]
        rows, cols, panel = block.shape
        pixels = rows * cols
        n = w_in.shape[0] // panel
        hidden = w_in.shape[1]
        chans = w_in.shape[0]
        lands = []
        for dr, dc in DIRS:
            lands.append(
                pltpu.VMEM((3 if dr else rows, EDGE if dc else cols, panel), BF16)
            )

        def sems(*dims):
            return [pltpu.SemaphoreType.DMA(dims), pltpu.SemaphoreType.DMA(dims)]

        padded = (rows + 6, cols + 2 * LEFT, panel)
        all_dims = (n, panel, pixels)
        normed_t, gall_t, hat, rstd, pad_x = call(
            front_kernel,
            "front",
            1,
            (
                shape(all_dims, BF16),
                shape(all_dims, BF16),
                shape((panel, pixels), F32),
                shape((1, pixels), F32),
                shape(padded, F32),
            ),
            lands
            + sems(8)
            + [pltpu.VMEM((pixels, 128), F32), pltpu.VMEM((n, 8, pixels), F32)]
            + sems(3, n - 1),
        )(block, kernel, grad_map)

        pre = mm(w_in, normed_t.reshape(chans, pixels), ((0,), (0,)))
        half = 0.5 * (1.0 + jax.scipy.special.erf(pre / jnp.sqrt(2.0)))
        act = (pre * half).astype(BF16)
        slope = half + pre * jnp.exp(-0.5 * pre * pre) / jnp.sqrt(2.0 * jnp.pi)
        d_act = mm(w_out, gall_t.reshape(chans, pixels), ((1,), (0,)))
        d_pre = (d_act * slope).astype(BF16)
        piece = chans // ny
        gdims = (2, ny, piece, hidden)
        tdims = (ny, 8, 128)
        output, grad_image, total, taps_total = call(
            back_kernel,
            "back",
            2,
            (
                shape(block.shape, BF16),
                shape(block.shape, BF16),
                shape(gdims, BF16),
                shape(tdims, F32),
            ),
            lands
            + sems(8)
            + [pltpu.VMEM((2, n - 1, panel, pixels), BF16), pltpu.VMEM((n, 8, pixels), F32)]
            + sems(3, n - 1)
            + [
                pltpu.VMEM((128, pixels), F32),
                pltpu.VMEM(block.shape, BF16),
                pltpu.VMEM(padded, F32),
                pltpu.VMEM(tdims, F32),
                pltpu.VMEM((ny, piece, hidden), BF16),
                pltpu.VMEM((ny, piece, hidden), BF16),
                pltpu.VMEM((2, ny // 2, piece, hidden), BF16),
                pltpu.VMEM((nz, piece, hidden), BF16),
                pltpu.VMEM(tdims, F32),
                pltpu.VMEM(tdims, F32),
                pltpu.VMEM((ny - 1, 8, 128), F32),
                pltpu.VMEM((nz, 8, 128), F32),
            ]
            + sems(9, ny)
            + sems(2, ny // 2, CHUNKS)
            + sems(ny, CHUNKS)
            + sems(2, ny // 2, CHUNKS)
            + sems(CHUNKS, nz - 1)
            + [
                pltpu.VMEM(all_dims, BF16),
                pltpu.VMEM(all_dims, BF16),
                pltpu.VMEM(gdims, BF16),
            ],
        )(
            w_in,
            w_out,
            act,
            d_pre,
            normed_t,
            gall_t,
            hat,
            rstd,
            block,
            grad_map,
            kernel,
            pad_x,
        )
        total = total.astype(F32)
        grad_in = total[0].reshape(chans, hidden)
        down = hidden // piece
        grad_out = jnp.concatenate(
            [total[1, k : k + down].reshape(hidden, hidden) for k in range(0, ny, down)], axis=1
        )
        grad_kernel = taps_total[:7, :7, :panel]
        return output[None], grad_image[None], grad_in, grad_out, grad_kernel

    return shards


def solution(mesh):
    ny = 8
    nz = mesh.shape["sp"] // (2 * ny)
    return jax.shard_map(
        make_shards(ny, nz),
        mesh=mesh,
        in_specs=(
            P("sp", None, None, "ch"),
            P("sp", None, None, "ch"),
            P(None, None, "ch"),
            P(None, "ch"),
            P("ch", None),
        ),
        out_specs=(
            P("sp", None, None, "ch"),
            P("sp", None, None, "ch"),
            P(None, "ch"),
            P("ch", None),
            P(None, None, "ch"),
        ),
        check_vma=False,
    )
```

```python
import jax
import jax.numpy as jnp
from jax import lax
from jax.experimental import pallas as pl
from jax.experimental.pallas import tpu as pltpu
from jax.sharding import PartitionSpec as P

GRID_W = 8
MESH = pl.DeviceIdType.MESH
DIRS = ((-1, 0), (1, 0), (0, -1), (0, 1), (-1, -1), (-1, 1), (1, -1), (1, 1))
EDGE = 16
LEFT = 8
CHUNKS = 3
F32 = jnp.float32
BF16 = jnp.bfloat16


def mm(a, b, dims):
    return lax.dot_general(a, b, (dims, ((), ())), preferred_element_type=F32)


def greet(peers, between=None):
    barrier = pltpu.get_barrier_semaphore()
    for peer in peers:
        pl.semaphore_signal(barrier, inc=1, device_id=peer, device_id_type=MESH)
    if between is not None:
        between()
    pl.semaphore_wait(barrier, len(peers))


def send(src, dst, send_sem, recv_sem, peer):
    copy = pltpu.make_async_remote_copy(
        src_ref=src,
        dst_ref=dst,
        send_sem=send_sem,
        recv_sem=recv_sem,
        device_id=peer,
        device_id_type=MESH,
    )
    copy.start()
    return copy


def call(body, name, cid, out_shape, scratch):
    def run(*args):
        return pl.pallas_call(
            body,
            out_shape=out_shape,
            in_specs=[pl.BlockSpec(memory_space=pltpu.VMEM)] * len(args),
            out_specs=tuple([pl.BlockSpec(memory_space=pltpu.VMEM)] * len(out_shape)),
            scratch_shapes=scratch,
            compiler_params=pltpu.CompilerParams(
                collective_id=cid, has_side_effects=True, vmem_limit_bytes=20 * 2**20
            ),
            name=name,
        )(*args)

    return run


def shape(dims, dtype):
    return jax.ShapeDtypeStruct(dims, dtype)


def window(dr, dc, rows, cols):
    r = slice(0, rows) if dr == 0 else (slice(0, 3) if dr < 0 else slice(rows - 3, rows))
    c = slice(0, cols) if dc == 0 else (slice(0, EDGE) if dc < 0 else slice(cols - EDGE, cols))
    return r, c


def margin_peers():
    b, ch = lax.axis_index("sp"), lax.axis_index("ch")
    row, col = b // GRID_W, b % GRID_W
    peers = []
    for dr, dc in DIRS:
        r = lax.rem(row + dr + GRID_W, GRID_W)
        c = lax.rem(col + dc + GRID_W, GRID_W)
        peers.append((r * GRID_W + c, ch))
    return peers


def start_margins(block, lands, send_sem, recv_sem, peers):
    rows, cols = block.shape[0], block.shape[1]
    copies = []
    for k, (dr, dc) in enumerate(DIRS):
        r, c = window(dr, dc, rows, cols)
        copies.append(
            send(block.at[r, c], lands[k], send_sem.at[k], recv_sem.at[k], peers[k])
        )
    return copies


def fill_margins(pad, block, lands):
    b = lax.axis_index("sp")
    row, col = b // GRID_W, b % GRID_W
    rows, cols = block.shape[0], block.shape[1]
    pad[3 : 3 + rows, LEFT : LEFT + cols] = block[...].astype(F32)
    for k, (dr, dc) in enumerate(DIRS):
        keep = jnp.logical_and(
            jnp.logical_and(row - dr >= 0, row - dr < GRID_W),
            jnp.logical_and(col - dc >= 0, col - dc < GRID_W),
        )
        value = lands[k][...].astype(F32)
        value = value * jnp.where(keep, 1.0, 0.0).astype(F32)
        if dc:
            value = value[:, :3] if dc < 0 else value[:, EDGE - 3 :]
        top = 3 if dr == 0 else (0 if dr > 0 else 3 + rows)
        left = LEFT if dc == 0 else (LEFT - 3 if dc > 0 else LEFT + cols)
        pad[top : top + value.shape[0], left : left + value.shape[1]] = value


def ch_peers(n):
    b, me = lax.axis_index("sp"), lax.axis_index("ch")
    return me, [(b, lax.rem(me + d, n)) for d in range(1, n)]


def send_stats(stat, me, peers, first, second, send_sem, recv_sem):
    stat[me, 0:1, :] = first
    stat[me, 1:2, :] = second
    return [
        send(stat.at[me], stat.at[me], send_sem.at[d], recv_sem.at[d], peer)
        for d, peer in enumerate(peers)
    ]


def sum_stats(stat, copies):
    for copy in copies:
        copy.wait()
    total = stat[0]
    for k in range(1, stat.shape[0]):
        total = total + stat[k]
    return total[0:1], total[1:2]


def to_channels(wide, panel):
    return wide[...].T[0:panel]


def to_pixels(tall, value, dims):
    rows, cols, panel = dims
    tall[0:panel, :] = value
    turned = tall[...].T
    return [turned[p * cols : (p + 1) * cols, 0:panel] for p in range(rows)]


def front_kernel(*refs):
    block, taps, grad_map = refs[0:3]
    normed_all, grad_all, hat, rstd, pad = refs[3:8]
    lands, msem, mrsem = refs[8:16], refs[16], refs[17]
    wide, stat, ssem, rsem = refs[18:22]
    rows, cols, panel = block.shape
    n = normed_all.shape[0]
    chans = n * panel
    me, peers = ch_peers(n)
    near = margin_peers()
    stat[me] = jnp.zeros(stat.shape[1:], F32)
    wide[...] = jnp.zeros_like(wide)
    for p in range(rows):
        wide[p * cols : (p + 1) * cols, 0:panel] = grad_map[p].astype(F32)
    grad_all[me] = to_channels(wide, panel).astype(BF16)
    greet(near + peers)
    copies = start_margins(block, lands, msem, mrsem, near)
    grads = [
        send(grad_all.at[me], grad_all.at[me], ssem.at[1, d], rsem.at[1, d], peer)
        for d, peer in enumerate(peers)
    ]
    pad[...] = jnp.zeros_like(pad)
    for copy in copies:
        copy.wait()
    fill_margins(pad, block, lands)
    rows_f = [taps[i].astype(F32) for i in range(7)]
    for p in range(rows):
        total = jnp.zeros(block.shape[1:], F32)
        for i in range(7):
            for j in range(7):
                start = LEFT - 3 + j
                total = total + rows_f[i][j : j + 1] * pad[p + i, start : start + cols, :]
        wide[p * cols : (p + 1) * cols, 0:panel] = total.astype(BF16).astype(F32)
    value = to_channels(wide, panel)
    stats = send_stats(
        stat,
        me,
        peers,
        jnp.sum(value, axis=0, keepdims=True),
        jnp.sum(value * value, axis=0, keepdims=True),
        ssem.at[0],
        rsem.at[0],
    )
    first, second = sum_stats(stat, stats)
    mean = first / chans
    var = second / chans - mean * mean
    scale = lax.rsqrt(var + 1e-06)
    rstd[...] = scale
    local = (value - mean) * scale
    hat[...] = local
    normed_all[me] = local.astype(BF16)
    outs = [
        send(normed_all.at[me], normed_all.at[me], ssem.at[2, d], rsem.at[2, d], peer)
        for d, peer in enumerate(peers)
    ]
    for copy in grads + outs:
        copy.wait()


def back_kernel(*refs):
    w_in, w_out, act, d_pre, normed_all, grad_all = refs[0:6]
    part_out, part_norm, grads = refs[52:55]
    hat, rstd, image, grad_map, taps, pad_x = refs[6:12]
    refs = refs[3:]
    output, grad_image, out, taps_out = refs[9:13]
    lands, msem, mrsem = refs[13:21], refs[21], refs[22]
    land, stat, csem, crsem, tall, d_conv, pad, mytaps = refs[23:31]
    land0, mine, land1, land2, tland0, tmine, tland1, tland2, ssem, rsem = refs[31:41]
    ring_send, ring_recv, pair_send, pair_recv = refs[41:45]
    sum_send, sum_recv, across_send, across_recv = refs[45:49]

    n, panel, pixels = part_out.shape
    rows, cols, _ = image.shape
    chans = n * panel
    b, ch = lax.axis_index("sp"), lax.axis_index("ch")
    me, peers = ch_peers(n)
    near = margin_peers()
    ny, nz = grads.shape[1], land2.shape[0]
    core, y, z = b % 2, (b // 2) % ny, b // (2 * ny)
    other = (b + 1 - 2 * core, ch)
    ys = [lax.rem(y + d, ny) for d in range(1, ny)]
    zs = [lax.rem(z + d, nz) for d in range(1, nz)]
    y_peers = [((z * ny + k) * 2 + core, ch) for k in ys]
    z_peers = [((k * ny + y) * 2 + core, ch) for k in zs]
    stat[me] = jnp.zeros(stat.shape[1:], F32)

    def first_products():
        part_norm[...] = (
            mm(w_in[...], d_pre[...], ((1,), (0,))).astype(BF16).reshape(part_norm.shape)
        )
        normed = normed_all[...].reshape(chans, pixels)
        grad_in = mm(normed, d_pre[...], ((1,), (1,))).astype(BF16)
        grads[0] = grad_in.reshape(grads.shape[1:])

    greet(peers + near + [other] + y_peers + z_peers, first_products)

    norms = [
        send(part_norm.at[peer[1]], land.at[0, d], csem.at[0, d], crsem.at[0, d], peer)
        for d, peer in enumerate(peers)
    ]
    hidden = act.shape[0]
    down = hidden // panel
    for k in range(0, n, down):
        panels = grad_all[k : k + down].reshape(hidden, pixels)
        grad_out = mm(act[...], panels, ((1,), (1,))).astype(BF16)
        grads[1, k : k + down] = grad_out.reshape(down, panel, hidden)
    half = ny // 2
    away = [half] + [a for d in range(half - 1, 0, -1) for a in (d, ny - d)] + [0]
    order = [lax.rem(y + a, ny) for a in away]
    firsts = [
        send(grads.at[1 - core, k], land0.at[k], ssem.at[0, d], rsem.at[0, d], other)
        for d, k in enumerate(order)
    ]
    part_out[...] = (
        mm(w_out[...], act[...], ((0,), (0,))).astype(BF16).reshape(part_out.shape)
    )
    outs = [
        send(part_out.at[peer[1]], land.at[1, d], csem.at[1, d], crsem.at[1, d], peer)
        for d, peer in enumerate(peers)
    ]
    tall[...] = jnp.zeros_like(tall)
    mytaps[...] = jnp.zeros_like(mytaps)
    pad[...] = jnp.zeros_like(pad)

    size = out.shape[2] // CHUNKS
    ring = [((z * ny + k) * 2 + core, ch) for k in (lax.rem(y + 1, ny), lax.rem(y + ny - 1, ny))]

    def take(d):
        k = order[d]
        firsts[d].wait()
        mine[k] = (grads[core, k].astype(F32) + land0[k].astype(F32)).astype(BF16)

    for d in range(3):
        take(d)
    sums, moves = {}, []
    for step in range(half + 1):
        for c in range(CHUNKS):
            part_rows = slice(c * size, (c + 1) * size)
            for way in range(2):
                reach = half if c % 2 == way else half - 1
                left = reach - step
                if left < 0:
                    continue
                k = lax.rem(y + (left if way == 0 else ny - left), ny)
                src = mine.at[k, part_rows]
                if step:
                    sums[way, step - 1, c].wait()
                    src = land1.at[way, step - 1, part_rows]
                if left and step:
                    src[...] = (src[...].astype(F32) + mine[k, part_rows].astype(F32)).astype(BF16)
                if left:
                    sums[way, step, c] = send(
                        src,
                        land1.at[way, step, part_rows],
                        sum_send.at[way, step, c],
                        sum_recv.at[way, step, c],
                        ring[way],
                    )
            if step == 0 and c == CHUNKS - 1:
                for d in range(3, ny):
                    take(d)
            if step == half:
                total = mine[y, part_rows].astype(F32)
                for way in range(2):
                    last = (half if c % 2 == way else half - 1) - 1
                    total = total + land1[way, last, part_rows].astype(F32)
                land2[z, part_rows] = total.astype(BF16)
                moves.append(
                    [
                        send(
                            land2.at[z, part_rows],
                            land2.at[z, part_rows],
                            across_send.at[c, d],
                            across_recv.at[c, d],
                            z_peers[d],
                        )
                        for d in range(nz - 1)
                    ]
                )

    d_norm = part_norm[me].astype(F32)
    for d, copy in enumerate(norms):
        copy.wait()
        d_norm = d_norm + land[0, d].astype(F32)
    local = hat[...]
    stats = send_stats(
        stat,
        me,
        peers,
        jnp.sum(d_norm, axis=0, keepdims=True),
        jnp.sum(d_norm * local, axis=0, keepdims=True),
        csem.at[2],
        crsem.at[2],
    )
    branch = part_out[me].astype(F32)
    for d, copy in enumerate(outs):
        copy.wait()
        branch = branch + land[1, d].astype(F32)
    for p, value in enumerate(to_pixels(tall, branch, image.shape)):
        output[p] = (image[p].astype(F32) + value).astype(BF16)
    first, second = sum_stats(stat, stats)
    back = rstd[...] * (d_norm - first / chans - local * second / chans)
    for p, value in enumerate(to_pixels(tall, back, image.shape)):
        d_conv[p] = value.astype(BF16)
    margins = start_margins(d_conv, lands, msem, mrsem, near)

    for i in range(7):
        for j in range(7):
            start = LEFT - 3 + j
            total = jnp.zeros(image.shape[1:], F32)
            for p in range(rows):
                total = total + d_conv[p].astype(F32) * pad_x[p + i, start : start + cols, :]
            mytaps[i, j : j + 1, 0:panel] = jnp.sum(total, axis=0, keepdims=True)
    tfirst = send(mytaps, tland0, ssem.at[1, 0], rsem.at[1, 0], other)

    def part(k, c):
        return out.at[core, k, c * size : (c + 1) * size]

    def pass_on(way, step, c, k):
        sems = ring_send.at[way, step, c], ring_recv.at[way, step, c]
        return send(part(k, c), part(k, c), *sems, ring[way])

    def share(step, c, k):
        return send(part(k, c), part(k, c), pair_send.at[step, c], pair_recv.at[step, c], other)

    def goes(way, step, c):
        return step < ny // 2 - 1 or (step == ny // 2 - 1 and c % 2 == way)

    flight, pairs = {}, []
    for c in range(CHUNKS):
        part_rows = slice(c * size, (c + 1) * size)
        for copy in moves[c]:
            copy.wait()
        total = land2[0, part_rows].astype(F32)
        for k in range(1, nz):
            total = total + land2[k, part_rows].astype(F32)
        out[core, y, part_rows] = total.astype(BF16)
        for way in range(2):
            flight[way, 0, c] = pass_on(way, 0, c, y)
        pairs.append(share(0, c, y))

    tfirst.wait()
    tmine[...] = mytaps[...] + tland0[...]
    tmoves = [
        send(tmine.at[ys[d]], tland1.at[d], ssem.at[3, d], rsem.at[3, d], y_peers[d])
        for d in range(ny - 1)
    ]

    for step in range(ny // 2):
        for c in range(CHUNKS):
            for way in range(2):
                if not goes(way, step, c):
                    continue
                flight[way, step, c].wait()
                away = step + 1
                k = lax.rem(y + (ny - away if way == 0 else away), ny)
                if goes(way, away, c):
                    flight[way, away, c] = pass_on(way, away, c, k)
                pairs.append(share(away if way == 0 else ny - away, c, k))
        if step == 0:
            ttotal = tmine[y]
            for d in range(ny - 1):
                tmoves[d].wait()
                ttotal = ttotal + tland1[d]
            tland2[z] = ttotal
            tmoves = [
                send(tland2.at[z], tland2.at[z], ssem.at[5, d], rsem.at[5, d], z_peers[d])
                for d in range(nz - 1)
            ]
        if step == 2:
            for copy in tmoves:
                copy.wait()
            ttotal = tland2[0]
            for k in range(1, nz):
                ttotal = ttotal + tland2[k]
            taps_out[y] = ttotal
            tmoves = [
                send(taps_out.at[y], taps_out.at[y], ssem.at[7, d], rsem.at[7, d], y_peers[d])
                for d in range(ny - 1)
            ]
    for copy in margins:
        copy.wait()
    fill_margins(pad, d_conv, lands)
    rows_f = [taps[i].astype(F32) for i in range(7)]
    for p in range(rows):
        total = grad_map[p].astype(F32)
        for i in range(7):
            for j in range(7):
                start = LEFT + 3 - j
                total = total + rows_f[i][j : j + 1] * pad[p + 6 - i, start : start + cols, :]
        grad_image[p] = total.astype(BF16)

    for copy in tmoves + pairs:
        copy.wait()


def make_shards(ny, nz):
    def shards(image, cotangent, kernel, w_in, w_out):
        block, grad_map = image[0], cotangent[0]
        rows, cols, panel = block.shape
        pixels = rows * cols
        n = w_in.shape[0] // panel
        hidden = w_in.shape[1]
        chans = w_in.shape[0]
        lands = []
        for dr, dc in DIRS:
            lands.append(
                pltpu.VMEM((3 if dr else rows, EDGE if dc else cols, panel), BF16)
            )

        def sems(*dims):
            return [pltpu.SemaphoreType.DMA(dims), pltpu.SemaphoreType.DMA(dims)]

        padded = (rows + 6, cols + 2 * LEFT, panel)
        all_dims = (n, panel, pixels)
        normed_t, gall_t, hat, rstd, pad_x = call(
            front_kernel,
            "front",
            1,
            (
                shape(all_dims, BF16),
                shape(all_dims, BF16),
                shape((panel, pixels), F32),
                shape((1, pixels), F32),
                shape(padded, F32),
            ),
            lands
            + sems(8)
            + [pltpu.VMEM((pixels, 128), F32), pltpu.VMEM((n, 8, pixels), F32)]
            + sems(3, n - 1),
        )(block, kernel, grad_map)

        pre = mm(w_in, normed_t.reshape(chans, pixels), ((0,), (0,)))
        half = 0.5 * (1.0 + jax.scipy.special.erf(pre / jnp.sqrt(2.0)))
        act = (pre * half).astype(BF16)
        slope = half + pre * jnp.exp(-0.5 * pre * pre) / jnp.sqrt(2.0 * jnp.pi)
        d_act = mm(w_out, gall_t.reshape(chans, pixels), ((1,), (0,)))
        d_pre = (d_act * slope).astype(BF16)
        piece = chans // ny
        gdims = (2, ny, piece, hidden)
        tdims = (ny, 8, 128)
        output, grad_image, total, taps_total = call(
            back_kernel,
            "back",
            2,
            (
                shape(block.shape, BF16),
                shape(block.shape, BF16),
                shape(gdims, BF16),
                shape(tdims, F32),
            ),
            lands
            + sems(8)
            + [pltpu.VMEM((2, n - 1, panel, pixels), BF16), pltpu.VMEM((n, 8, pixels), F32)]
            + sems(3, n - 1)
            + [
                pltpu.VMEM((128, pixels), F32),
                pltpu.VMEM(block.shape, BF16),
                pltpu.VMEM(padded, F32),
                pltpu.VMEM(tdims, F32),
                pltpu.VMEM((ny, piece, hidden), BF16),
                pltpu.VMEM((ny, piece, hidden), BF16),
                pltpu.VMEM((2, ny // 2, piece, hidden), BF16),
                pltpu.VMEM((nz, piece, hidden), BF16),
                pltpu.VMEM(tdims, F32),
                pltpu.VMEM(tdims, F32),
                pltpu.VMEM((ny - 1, 8, 128), F32),
                pltpu.VMEM((nz, 8, 128), F32),
            ]
            + sems(9, ny)
            + sems(2, ny // 2, CHUNKS)
            + sems(ny, CHUNKS)
            + sems(2, ny // 2, CHUNKS)
            + sems(CHUNKS, nz - 1)
            + [
                pltpu.VMEM(all_dims, BF16),
                pltpu.VMEM(all_dims, BF16),
                pltpu.VMEM(gdims, BF16),
            ],
        )(
            w_in,
            w_out,
            act,
            d_pre,
            normed_t,
            gall_t,
            hat,
            rstd,
            block,
            grad_map,
            kernel,
            pad_x,
        )
        total = total.astype(F32)
        grad_in = total[0].reshape(chans, hidden)
        down = hidden // piece
        grad_out = jnp.concatenate(
            [total[1, k : k + down].reshape(hidden, hidden) for k in range(0, ny, down)], axis=1
        )
        grad_kernel = taps_total[:7, :7, :panel]
        return output[None], grad_image[None], grad_in, grad_out, grad_kernel

    return shards


def solution(mesh):
    ny = 8
    nz = mesh.shape["sp"] // (2 * ny)
    return jax.shard_map(
        make_shards(ny, nz),
        mesh=mesh,
        in_specs=(
            P("sp", None, None, "ch"),
            P("sp", None, None, "ch"),
            P(None, None, "ch"),
            P(None, "ch"),
            P("ch", None),
        ),
        out_specs=(
            P("sp", None, None, "ch"),
            P("sp", None, None, "ch"),
            P(None, "ch"),
            P("ch", None),
            P(None, None, "ch"),
        ),
        check_vma=False,
    )
```
